32 devices in a mesh: grp: 16 (over z, x, core), dev: 2 (over y).
Axes of the slice: x: 2, y: 2, z: 4, core: 2. Of those that a mesh axis runs over, the one named last changes fastest.
Arguments:
- tokens: bfloat16 [2048, 768], P(('grp', 'dev')), may hold values from -6 to 6
- expert_ids: int32 [2048, 8], P(('grp', 'dev')), may hold values from 0 to 31, as said below
- gates: bfloat16 [2048, 8], P(('grp', 'dev')), may hold values from 0.099609375 to 0.5
- w_in: bfloat16 [32, 768, 1536], P(('grp', 'dev')), may hold values from -0.21875 to 0.21875
- w_out: bfloat16 [32, 1536, 768], P(('grp', 'dev')), may hold values from -0.15625 to 0.15625
Outputs:
- mixed: bfloat16 [2048, 768], P(('grp', 'dev'))
The draws below stay inside these ranges and needn't reach their ends.
Inputs may be any that keep to these rules, and one draw needn't show every extreme that they name: `expert_ids`: row t lists 8 experts; columns 2 * k and 2 * k + 1 are two different experts of one group (experts g * 2 to g * 2 + 1 form group g), and the four groups of a row differ. The owner of token t is t // 64, and its dev index is the owner modulo 2. The tokens of one owner pick one group at most 48 times, and every owner reaches it for some group. The tokens whose owners share a dev index pick each group exactly 4 * 64 times in all and each expert at most 256 times; in every group one expert is picked 256 times by the tokens of every dev index.
All inputs are finite; a program needn't handle non-finite values.
Results may differ from the reference program's by a relative error of at most 0.0057.
Values may be sent and summed in bfloat16 or wider, within the bound.
No kernel may reach another device: no remote copies, remote signals or barrier semaphores. Data moves between devices by JAX's collectives and lax.ppermute only.
A program may use at most 64 MiB of HBM per device.

```python
import jax
import jax.numpy as jnp
from jax import lax

D = 768
FF = 1536
PICKS = 8
TOK_DEV = 64
EXPERTS = 32
TOKENS = 2048
CAP_G = 48
CAP_E = 256
N_GRP = 16
N_DEV = 2


def draw_expert_ids(key, part):
    slots = 4 * TOK_DEV
    base = jax.random.fold_in(key, 11)
    key_shift, key_group, key_hot, key_rest = jax.random.split(base, 4)
    shift_perm = jax.vmap(lambda sub: jax.random.permutation(sub, N_GRP))(jax.random.split(key_shift, N_DEV))
    group_perm = jax.random.permutation(key_group, N_GRP)
    group_inverse = jnp.argsort(group_perm)
    hot_expert = jax.random.randint(key_hot, (N_GRP,), 0, N_DEV)
    rest_perm = jax.vmap(lambda sub: jax.random.permutation(sub, N_DEV - 1))(jax.random.split(key_rest, N_GRP * N_DEV))
    rest_perm = rest_perm.reshape(N_GRP, N_DEV, N_DEV - 1) + 1
    rotation = jnp.concatenate([jnp.zeros((N_GRP, N_DEV, 1), jnp.int32), rest_perm.astype(jnp.int32)], axis=2)
    run_index = (group_inverse[None, :, None] - shift_perm[:, None, :]) % N_GRP
    run_length = jnp.clip(slots - run_index * CAP_G, 0, CAP_G)
    prefix = jnp.cumsum(run_length, axis=2) - run_length
    source_grp = jnp.arange(N_GRP)[:, None, None]
    source_dev = jnp.arange(N_DEV)[None, :, None]
    slot_index = jnp.arange(slots)[None, None, :]
    slot_run = slot_index // CAP_G
    rotated = (slot_run + shift_perm[source_dev, source_grp]) % N_GRP
    relay_group = group_perm[rotated]
    relay_row = prefix[source_dev, relay_group, source_grp] + slot_index % CAP_G
    bounds = CAP_E + (jnp.arange(1, N_DEV) - 1) * (2 * slots - CAP_E) // (N_DEV - 1)

    def expert_of(position):
        run_number = jnp.sum((position[..., None] >= bounds).astype(jnp.int32), axis=-1)
        return (hot_expert[relay_group] + rotation[relay_group, source_dev, run_number]) % N_DEV
    first_pick = relay_group * N_DEV + expert_of(relay_row)
    second_pick = relay_group * N_DEV + expert_of(relay_row + slots)
    stacked = jnp.stack([first_pick, second_pick], axis=-1)
    stacked = stacked.reshape(N_GRP, N_DEV, 4, TOK_DEV, 2).transpose(0, 1, 3, 2, 4)
    return stacked.reshape(N_GRP * N_DEV * TOK_DEV, 8).astype(jnp.int32)


def level_of(stream_key, extent, shards, least, high):
    def one(dim, parts):
        steps = jax.random.uniform(jax.random.fold_in(jax.random.fold_in(stream_key, 6), dim), (parts,), jnp.float32, least / len(shards), high / len(shards))
        return jnp.repeat(jnp.exp(steps), extent[dim] // parts).reshape((-1,) + (1,) * (len(extent) - dim - 1))

    loudness = one(*shards[0])
    for cut in shards[1:]:
        loudness = loudness * one(*cut)
    return loudness


def normal_values(key, shape, deviation, bound, pieces=(), held_as=jnp.bfloat16):
    entries = jax.random.normal(key, shape, jnp.float32) * deviation
    if len(pieces) > 0:
        entries = level_of(key, shape, pieces, -0.22, 0.18) * entries
    return jnp.clip(entries, min=-bound, max=bound).astype(held_as)


def setup_inputs(seed: int = 0) -> dict:
    seeds = jax.random.split(jax.random.key(seed), 6)
    return {
        "tokens": normal_values(seeds[0], (TOKENS, D), 1.0, 6.0, ((0, 32),)),
        "expert_ids": draw_expert_ids(jax.random.fold_in(seeds[5], 71), 0),
        "gates": jnp.clip(0.099609375 + 0.40039062 * jax.random.uniform(seeds[2], (TOKENS, PICKS), jnp.float32) ** level_of(seeds[2], (TOKENS, PICKS), ((0, 32),), -0.2, 0.2), 0.099609375, 0.5).astype(jnp.bfloat16),
        "w_in": normal_values(seeds[3], (EXPERTS, D, FF), D ** -0.5, 0.21875, ((0, 32),)),
        "w_out": normal_values(seeds[4], (EXPERTS, FF, D), FF ** -0.5, 0.15625, ((0, 32),)),
    }


def reference(tokens, expert_ids, gates, w_in, w_out):
    flat_ids = expert_ids.reshape(-1)
    flat_gates = gates.reshape(-1).astype(jnp.float32)
    pair_total = flat_ids.shape[0]
    capacity = N_DEV * CAP_E

    def expert_step(running, expert):
        picked = jnp.nonzero(flat_ids == expert, size=capacity, fill_value=pair_total)[0].astype(jnp.int32)
        in_range = picked < pair_total
        token_rows = jnp.minimum(picked // PICKS, TOKENS - 1).astype(jnp.int32)
        gathered = jnp.take(tokens, token_rows, axis=0).astype(jnp.float32)
        hidden = jnp.maximum(jnp.dot(gathered, w_in[expert].astype(jnp.float32), preferred_element_type=jnp.float32), 0.0).astype(jnp.bfloat16)
        output = jnp.dot(hidden.astype(jnp.float32), w_out[expert].astype(jnp.float32), preferred_element_type=jnp.float32).astype(jnp.bfloat16)
        weights_row = jnp.where(in_range, jnp.take(flat_gates, jnp.minimum(picked, pair_total - 1).astype(jnp.int32)), 0.0)
        running = running.at[token_rows].add(weights_row[:, None] * output.astype(jnp.float32))
        return running, None

    start = jnp.zeros((TOKENS, D), jnp.float32)
    running, unused = lax.scan(expert_step, start, jnp.arange(EXPERTS, dtype=jnp.int32))
    return running.astype(jnp.bfloat16)
```

```python
import functools

import jax
import jax.numpy as jnp
from jax import lax
from jax.experimental import pallas as pl
from jax.experimental.pallas import tpu as pltpu
from jax.sharding import PartitionSpec as P

LANES = 128
SUB = 8


class Rings:
    def __init__(self, length, rounds, clockwise, counter, mirror, partner):
        self.length = length
        self.rounds = rounds
        self.perms = (clockwise, counter, mirror)
        self.partner = partner


def wrap(step, length):
    step %= length
    return step - length if step > length // 2 else step


def seen_from_source(channel, block, length):
    step, plane = block
    if channel == 0:
        return (wrap(step + 1, length), plane)
    if channel == 1:
        return (wrap(step - 1, length), plane)
    return (step, 1 - plane)


def gather_rounds(length):
    everything = [(wrap(s, length), p) for p in range(2) for s in range(length)]
    everything.sort(key=lambda b: (b[1], abs(b[0]), -b[0]))
    held = {(0, 0)}
    rounds = []
    while len(held) < len(everything):
        chosen = {}
        for channel in range(3):
            for block in everything:
                if block in held or block in chosen.values():
                    continue
                if channel == 2 and block[1] == 0:
                    continue
                if seen_from_source(channel, block, length) in held:
                    chosen[channel] = block
                    break
        rounds.append(chosen)
        held |= set(chosen.values())
    return rounds


def find_rings(mesh):
    grid = mesh.devices
    n_grp, n_dev = grid.shape
    if n_dev != 2 or not hasattr(grid[0, 0], "coords"):
        return None
    place = {}
    for g in range(n_grp):
        for d in range(n_dev):
            device = grid[g, d]
            place[(tuple(device.coords), device.core_on_chip)] = (g, d)
    planes = []
    for d in range(n_dev):
        planes.append(sorted({tuple(grid[g, d].coords) for g in range(n_grp)}))
    if 2 * len(planes[0]) != n_grp or set(planes[0]) & set(planes[1]):
        return None
    wide = [a for a in range(3) if len({c[a] for c in planes[0]}) == 2]
    flat = [a for a in range(3) if len({c[a] for c in planes[0]}) == 1]
    if not wide or len(flat) != 1:
        return None
    side = wide[0]
    along = [a for a in range(3) if a not in (side, flat[0])][0]
    low = min(c[side] for c in planes[0])
    up = sorted((c for c in planes[0] if c[side] == low), key=lambda c: c[along])
    down = sorted((c for c in planes[0] if c[side] != low), key=lambda c: -c[along])
    order = up + down
    length = len(order)

    def index(chip, core):
        g, d = place[(chip, core)]
        return g * n_dev + d

    def mirrored(chip):
        other = planes[1][0][flat[0]]
        return tuple(other if a == flat[0] else v for a, v in enumerate(chip))

    if any((mirrored(c), k) not in place or (c, k) not in place for c in order for k in range(2)):
        return None
    if any(place[(c, k)][0] != place[(mirrored(c), k)][0] for c in order for k in range(2)):
        return None
    clockwise, counter, mirror, partner = [], [], [], []
    for here in range(length):
        after = (here + 1) % length
        for core in range(2):
            for turn in (lambda c: c, mirrored):
                a, b = index(turn(order[here]), core), index(turn(order[after]), core)
                clockwise.append((a, b))
                counter.append((b, a))
                partner.append((a, index(turn(order[here]), 1 - core)))
            a, b = index(order[here], core), index(mirrored(order[here]), core)
            mirror += [(a, b), (b, a)]
    return Rings(length, gather_rounds(length), clockwise, counter, mirror, partner)


def pack_kernel(ids_ref, gates_ref, tokens_ref, out_ref, *, experts):
    count, width = tokens_ref.shape
    picks = ids_ref.shape[1]
    out_ref[:count, :] = tokens_ref[...]
    ids = ids_ref[...]
    gates = gates_ref[...].astype(jnp.float32)
    column = lax.broadcasted_iota(jnp.int32, (count, experts), 1)
    table = jnp.zeros((count, experts), jnp.float32)
    for k in range(picks):
        table += jnp.where(ids[:, k : k + 1] == column, gates[:, k : k + 1], 0.0)
    lane = lax.broadcasted_iota(jnp.int32, (count, LANES), 1)
    row = lax.broadcasted_iota(jnp.int32, (count, LANES), 0)
    twice = ((lane & (count - 1)) == row).astype(jnp.bfloat16)
    turned = lax.dot_general(
        table.astype(jnp.bfloat16),
        twice,
        (((0,), (0,)), ((), ())),
        preferred_element_type=jnp.float32,
    ).astype(jnp.bfloat16)
    out_ref[count:, :] = jnp.zeros((SUB, width), jnp.bfloat16)
    for q in range(experts // SUB):
        out_ref[count:, q * LANES : (q + 1) * LANES] = turned[q * SUB : (q + 1) * SUB, :]


def pack(ids, gates, tokens, experts):
    count, width = tokens.shape
    return pl.pallas_call(
        functools.partial(pack_kernel, experts=experts),
        out_shape=jax.ShapeDtypeStruct((count + SUB, width), jnp.bfloat16),
        name="pack",
    )(ids, gates, tokens)


def expert_kernel(*refs, pairs, count, cap):
    expert_ref = refs[0]
    blocks = refs[1 : 1 + 2 * pairs]
    w_in_ref, w_out_ref = refs[1 + 2 * pairs : 3 + 2 * pairs]
    keep_ref, give_ref = refs[3 + 2 * pairs : 5 + 2 * pairs]
    rows, tails, w_first, w_second, kept, given, in_sem, w_sem, out_sem = refs[5 + 2 * pairs :]
    both = 2 * count
    half = pairs // 2
    width = rows.shape[1]
    tail_copies = []
    row_copies = []
    for b in range(2 * pairs):
        tail_copies.append(
            pltpu.make_async_copy(
                blocks[b].at[pl.ds(count, SUB)], tails.at[pl.ds(b * SUB, SUB)], in_sem.at[0, b]
            )
        )
        row_copies.append(
            pltpu.make_async_copy(
                blocks[b].at[pl.ds(0, count)], rows.at[pl.ds(b * count, count)], in_sem.at[1, b]
            )
        )
    for copy in tail_copies:
        copy.start()
    for copy in row_copies:
        copy.start()
    first_copy = pltpu.make_async_copy(w_in_ref.at[0], w_first, w_sem.at[0])
    second_copy = pltpu.make_async_copy(w_out_ref.at[0], w_second, w_sem.at[1])
    first_copy.start()
    second_copy.start()

    expert = expert_ref[0]
    sub = expert % SUB
    group = expert // SUB
    for copy in tail_copies:
        copy.wait()
    table = tails[:, pl.ds(pl.multiple_of(group * LANES, LANES), LANES)]
    row_of = lax.broadcasted_iota(jnp.int32, (pairs, 2 * pairs * SUB), 0)
    col_of = lax.broadcasted_iota(jnp.int32, (pairs, 2 * pairs * SUB), 1)
    pick_a = (col_of == (2 * row_of) * SUB + sub).astype(jnp.bfloat16)
    pick_b = (col_of == (2 * row_of + 1) * SUB + sub).astype(jnp.bfloat16)
    dot = functools.partial(jnp.dot, preferred_element_type=jnp.float32)
    gate_a = dot(pick_a, table)
    gate_b = dot(pick_b, table)
    lane = lax.broadcasted_iota(jnp.int32, (pairs, LANES), 1)
    gate = jnp.where(lane < count, gate_a, gate_b)
    chosen = gate > 0.0
    ones = chosen.astype(jnp.bfloat16)
    upper = (
        lax.broadcasted_iota(jnp.int32, (LANES, LANES), 0)
        < lax.broadcasted_iota(jnp.int32, (LANES, LANES), 1)
    ).astype(jnp.bfloat16)
    inside = dot(ones, upper)
    left = lax.broadcasted_iota(jnp.int32, (pairs, pairs), 0)
    right = lax.broadcasted_iota(jnp.int32, (pairs, pairs), 1)
    before = ((right < left) & (right // half == left // half)).astype(jnp.bfloat16)
    total = jnp.sum(ones.astype(jnp.float32), axis=1, keepdims=True)
    offset = dot(before, jnp.broadcast_to(total, (pairs, LANES)).astype(jnp.bfloat16))
    seat = jnp.where(chosen, inside + offset, -1.0).astype(jnp.int32)

    place = []
    for p in range(2):
        seats = lax.broadcasted_iota(jnp.int32, (cap, LANES), 0)
        hot = [
            (seats == seat[p * half + o : p * half + o + 1, :]).astype(jnp.bfloat16)
            for o in range(half)
        ]
        weighted = [
            hot[o] * gate[p * half + o : p * half + o + 1, :].astype(jnp.bfloat16)
            for o in range(half)
        ]
        place.append((jnp.concatenate(hot, axis=1), jnp.concatenate(weighted, axis=1)))
    for copy in row_copies:
        copy.wait()
    span = half * both
    taken = [
        dot(place[p][0], rows[p * span : (p + 1) * span, :]).astype(jnp.bfloat16) for p in range(2)
    ]
    taken = jnp.concatenate(taken, axis=0)
    first_copy.wait()
    hidden = jnp.maximum(dot(taken, w_first[...]), 0.0).astype(jnp.bfloat16)
    second_copy.wait()
    result = dot(hidden, w_second[...]).astype(jnp.bfloat16)
    out_copies = []
    for p in range(2):
        spread = lax.dot_general(
            place[p][1],
            result[p * cap : (p + 1) * cap, :],
            (((0,), (0,)), ((), ())),
            preferred_element_type=jnp.float32,
        ).astype(jnp.bfloat16)
        for o in range(half):
            at = p * half + o
            kept[at] = spread[o * both : o * both + count, :]
            given[at] = spread[o * both + count : (o + 1) * both, :]
        for k, (store, target) in enumerate(((kept, keep_ref), (given, give_ref))):
            copy = pltpu.make_async_copy(
                store.at[pl.ds(p * half, half)],
                target.at[pl.ds(p * half, half)],
                out_sem.at[p, k],
            )
            copy.start()
            out_copies.append(copy)
    for copy in out_copies:
        copy.wait()


def expert_call(expert, blocks, w_in, w_out, count, cap):
    pairs = len(blocks) // 2
    width = blocks[0].shape[1]
    units = w_in.shape[2]
    anywhere = pl.BlockSpec(memory_space=pl.ANY)
    out = jax.ShapeDtypeStruct((pairs, count, width), jnp.bfloat16)
    return pl.pallas_call(
        functools.partial(expert_kernel, pairs=pairs, count=count, cap=cap),
        in_specs=[pl.BlockSpec(memory_space=pltpu.SMEM)] + [anywhere] * (len(blocks) + 2),
        out_specs=[anywhere, anywhere],
        out_shape=[out, out],
        scratch_shapes=[
            pltpu.VMEM((2 * pairs * count, width), jnp.bfloat16),
            pltpu.VMEM((2 * pairs * SUB, width), jnp.bfloat16),
            pltpu.VMEM((width, units), jnp.bfloat16),
            pltpu.VMEM((units, width), jnp.bfloat16),
            pltpu.VMEM((pairs, count, width), jnp.bfloat16),
            pltpu.VMEM((pairs, count, width), jnp.bfloat16),
            pltpu.SemaphoreType.DMA((2, 2 * pairs)),
            pltpu.SemaphoreType.DMA((2,)),
            pltpu.SemaphoreType.DMA((2, 2)),
        ],
        name="expert",
    )(expert, *blocks, w_in, w_out)


def on_rings(rings, tokens, expert_ids, gates, w_in, w_out):
    axes = ("grp", "dev")
    n_dev = lax.axis_size("dev")
    experts = lax.axis_size("grp") * n_dev
    count, width = tokens.shape
    if 2 * count != LANES or experts % SUB or experts * LANES > SUB * width:
        return per_device(tokens, expert_ids, gates, w_in, w_out)
    length = rings.length
    inverse = (rings.perms[1], rings.perms[0], rings.perms[2])
    own = pack(expert_ids, gates, tokens, experts)
    held = {(0, 0): own}
    twin = {(0, 0): lax.ppermute(own, axes, rings.partner)}
    for chosen in rings.rounds:
        fresh = {}
        for channel, block in chosen.items():
            source = held[seen_from_source(channel, block, length)]
            fresh[block] = lax.ppermute(source, axes, rings.perms[channel])
        for block, value in fresh.items():
            twin[block] = lax.ppermute(value, axes, rings.partner)
        held.update(fresh)
    order = sorted(held, key=lambda b: (b[1], b[0]))
    blocks = [side[b] for b in order for side in (held, twin)]
    expert = (lax.axis_index("grp") * n_dev + lax.axis_index("dev")).astype(jnp.int32).reshape(1)
    cap = min(4 * count, length * 2 * count)
    keep, give = expert_call(expert, blocks, w_in, w_out, count, cap)
    back = lax.ppermute(give, axes, rings.partner)
    parts = {b: [keep[i], back[i]] for i, b in enumerate(order)}

    def total(block):
        value = parts[block][0].astype(jnp.float32)
        for other in parts[block][1:]:
            value = value + other.astype(jnp.float32)
        return value.astype(jnp.bfloat16)

    for chosen in reversed(rings.rounds):
        arrived = []
        for channel, block in chosen.items():
            value = lax.ppermute(total(block), axes, inverse[channel])
            arrived.append((seen_from_source(channel, block, length), value))
        for block, value in arrived:
            parts[block].append(value)
    return total((0, 0))


def earlier_count(onehot):
    return jnp.cumsum(onehot, axis=0) - onehot


def contract_rows(left, right):
    return lax.dot_general(
        left,
        right,
        (((0,), (0,)), ((), ())),
        precision=lax.Precision.HIGHEST,
        preferred_element_type=jnp.float32,
    )


def expert_rows(slot_block, w_first, w_second):

    def one_block(rows_block):
        hidden = jnp.maximum(
            jnp.dot(rows_block, w_first, preferred_element_type=jnp.float32), 0.0
        ).astype(jnp.bfloat16)
        return jnp.dot(hidden, w_second, preferred_element_type=jnp.float32).astype(jnp.bfloat16)

    return lax.map(one_block, slot_block)


def seat_sources(seat_of, valid, seat_total):
    item_count = seat_of.shape[0]
    target_seat = jnp.where(valid, seat_of, seat_total)
    empty_seats = jnp.full((seat_total,), item_count, jnp.int32)
    return empty_seats.at[target_seat].set(jnp.arange(item_count, dtype=jnp.int32), mode="drop")


def per_device(tokens, expert_ids, gates, w_in, w_out):
    n_grp = lax.axis_size("grp")
    n_dev = lax.axis_size("dev")
    token_count, feature_width = tokens.shape
    cap_grp = min(token_count, 3 * ((4 * token_count + n_grp - 1) // n_grp))
    cap_exp = min(4 * token_count, 24 * token_count // n_dev)
    seat_total = n_dev * cap_exp
    zero_half = jnp.zeros((), jnp.bfloat16)
    w_first = w_in[0]
    w_second = w_out[0]
    pair_ids = expert_ids.reshape(token_count * 4, 2)
    pair_group = pair_ids[:, 0] // n_dev
    group_hot = (pair_group[:, None] == jnp.arange(n_grp)[None, :]).astype(jnp.int32)
    group_rank = jnp.sum(earlier_count(group_hot) * group_hot, axis=1)
    target = pair_group * cap_grp + group_rank
    slot_count = n_grp * cap_grp
    placed = (target[None, :] == jnp.arange(slot_count)[:, None]).astype(jnp.int32)
    token_hot = placed.reshape(slot_count, token_count, 4).sum(axis=2)
    rows_out = jnp.dot(
        token_hot.astype(jnp.bfloat16), tokens, preferred_element_type=jnp.float32
    ).astype(jnp.bfloat16)
    local_ids = pair_ids % n_dev
    picks_out = jnp.dot(placed, local_ids + 1) - 1
    gains_out = jnp.dot(
        placed.astype(jnp.bfloat16),
        gates.reshape(token_count * 4, 2),
        preferred_element_type=jnp.float32,
    ).astype(jnp.bfloat16)
    rows_in, picks_in, gains_in = (
        lax.all_to_all(
            rows_out.reshape(n_grp, cap_grp, feature_width),
            "grp",
            split_axis=0,
            concat_axis=0,
            tiled=True,
        ),
        lax.all_to_all(
            picks_out.reshape(n_grp, cap_grp, 2), "grp", split_axis=0, concat_axis=0, tiled=True
        ),
        lax.all_to_all(
            gains_out.reshape(n_grp, cap_grp, 2), "grp", split_axis=0, concat_axis=0, tiled=True
        ),
    )
    relay_rows = rows_in.reshape(slot_count, feature_width)
    relay_picks = picks_in.reshape(slot_count, 2)
    relay_gains = gains_in.reshape(slot_count, 2)
    live_count = 4 * token_count
    slot_live = (relay_picks[:, 0] >= 0).astype(jnp.int32)
    slot_order = jnp.cumsum(slot_live) - 1
    packed = (
        (slot_order[None, :] == jnp.arange(live_count)[:, None]) & (slot_live[None, :] > 0)
    ).astype(jnp.int32)
    packed_rows = jnp.dot(
        packed.astype(jnp.bfloat16), relay_rows, preferred_element_type=jnp.float32
    ).astype(jnp.bfloat16)
    packed_picks = jnp.dot(packed, relay_picks)
    packed_gains = jnp.dot(
        packed.astype(jnp.bfloat16), relay_gains, preferred_element_type=jnp.float32
    ).astype(jnp.bfloat16)
    group_rows, group_picks, group_gains = (
        lax.all_gather(packed_rows, "dev", axis=0, tiled=True),
        lax.all_gather(packed_picks, "dev", axis=0, tiled=True),
        lax.all_gather(packed_gains, "dev", axis=0, tiled=True),
    )
    gathered_count = group_rows.shape[0]
    chosen = jnp.sum((group_picks == lax.axis_index("dev")).astype(jnp.int32), axis=1)
    expert_seat = jnp.cumsum(chosen) - 1
    seat_source = seat_sources(expert_seat, chosen > 0, seat_total)
    seat_live = seat_source < gathered_count
    taken_rows = jnp.take(group_rows, jnp.minimum(seat_source, gathered_count - 1), axis=0)
    expert_in = jnp.where(seat_live[:, None], taken_rows, zero_half)
    expert_out = expert_rows(
        expert_in.reshape(n_dev, cap_exp, feature_width), w_first, w_second
    ).reshape(seat_total, feature_width)
    spread_rows = jnp.take(expert_out, jnp.clip(expert_seat, 0, seat_total - 1), axis=0)
    spread = jnp.where((chosen > 0)[:, None], spread_rows, zero_half)
    back = lax.all_to_all(
        spread.reshape(n_dev, live_count, feature_width),
        "dev",
        split_axis=0,
        concat_axis=0,
        tiled=True,
    )
    match = (packed_picks[None, :, :] == jnp.arange(n_dev)[:, None, None]).astype(jnp.float32)
    row_weights = jnp.sum(match * packed_gains.astype(jnp.float32)[None, :, :], axis=2)
    packed_sum = jnp.sum(row_weights[:, :, None] * back.astype(jnp.float32), axis=0)
    partial_value = contract_rows(packed.astype(jnp.float32), packed_sum)
    returned_sums = lax.all_to_all(
        partial_value.reshape(n_grp, cap_grp, feature_width),
        "grp",
        split_axis=0,
        concat_axis=0,
        tiled=True,
    )
    mixed = contract_rows(
        token_hot.astype(jnp.float32), returned_sums.reshape(slot_count, feature_width)
    )
    return mixed.astype(jnp.bfloat16)


def solution(mesh):
    rings = find_rings(mesh)
    body = per_device if rings is None else functools.partial(on_rings, rings)
    return jax.shard_map(
        body,
        mesh=mesh,
        in_specs=(
            P(("grp", "dev"), None),
            P(("grp", "dev"), None),
            P(("grp", "dev"), None),
            P(("grp", "dev"), None, None),
            P(("grp", "dev"), None, None),
        ),
        out_specs=P(("grp", "dev"), None),
        check_vma=False,
    )
```

```python
import functools

import jax
import jax.numpy as jnp
import numpy as np
from jax import lax
from jax.experimental import pallas as pl
from jax.experimental.pallas import tpu as pltpu
from jax.sharding import PartitionSpec as P

LANES = 128
SUB = 8


class Rings:
    def __init__(self, length, rounds, clockwise, counter, mirror, partner, cores):
        self.length = length
        self.rounds = rounds
        self.perms = (clockwise, counter, mirror)
        self.partner = partner
        self.mates = [mate for _, mate in sorted(partner)]
        self.cores = cores


def wrap(step, length):
    step %= length
    return step - length if step > length // 2 else step


def seen_from_source(channel, block, length):
    step, plane = block
    if channel == 0:
        return (wrap(step + 1, length), plane)
    if channel == 1:
        return (wrap(step - 1, length), plane)
    return (step, 1 - plane)


def gather_rounds(length):
    everything = [(wrap(s, length), p) for p in range(2) for s in range(length)]
    everything.sort(key=lambda b: (b[1], abs(b[0]), -b[0]))
    held = {(0, 0)}
    rounds = []
    while len(held) < len(everything):
        chosen = {}
        for channel in range(3):
            for block in everything:
                if block in held or block in chosen.values():
                    continue
                if channel == 2 and block[1] == 0:
                    continue
                if seen_from_source(channel, block, length) in held:
                    chosen[channel] = block
                    break
        rounds.append(chosen)
        held |= set(chosen.values())
    return rounds


def find_rings(mesh):
    grid = mesh.devices
    n_grp, n_dev = grid.shape
    if n_dev != 2 or not hasattr(grid[0, 0], "coords"):
        return None
    place = {}
    for g in range(n_grp):
        for d in range(n_dev):
            device = grid[g, d]
            place[(tuple(device.coords), device.core_on_chip)] = (g, d)
    planes = []
    for d in range(n_dev):
        planes.append(sorted({tuple(grid[g, d].coords) for g in range(n_grp)}))
    if 2 * len(planes[0]) != n_grp or set(planes[0]) & set(planes[1]):
        return None
    wide = [a for a in range(3) if len({c[a] for c in planes[0]}) == 2]
    flat = [a for a in range(3) if len({c[a] for c in planes[0]}) == 1]
    if not wide or len(flat) != 1:
        return None
    side = wide[0]
    along = [a for a in range(3) if a not in (side, flat[0])][0]
    low = min(c[side] for c in planes[0])
    up = sorted((c for c in planes[0] if c[side] == low), key=lambda c: c[along])
    down = sorted((c for c in planes[0] if c[side] != low), key=lambda c: -c[along])
    order = up + down
    length = len(order)

    def index(chip, core):
        g, d = place[(chip, core)]
        return g * n_dev + d

    def mirrored(chip):
        other = planes[1][0][flat[0]]
        return tuple(other if a == flat[0] else v for a, v in enumerate(chip))

    if any((mirrored(c), k) not in place or (c, k) not in place for c in order for k in range(2)):
        return None
    if any(place[(c, k)][0] != place[(mirrored(c), k)][0] for c in order for k in range(2)):
        return None
    clockwise, counter, mirror, partner = [], [], [], []
    for here in range(length):
        after = (here + 1) % length
        for core in range(2):
            for turn in (lambda c: c, mirrored):
                a, b = index(turn(order[here]), core), index(turn(order[after]), core)
                clockwise.append((a, b))
                counter.append((b, a))
                partner.append((a, index(turn(order[here]), 1 - core)))
            a, b = index(order[here], core), index(mirrored(order[here]), core)
            mirror += [(a, b), (b, a)]
    cores = [device.core_on_chip for device in grid.flat]
    return Rings(length, gather_rounds(length), clockwise, counter, mirror, partner, cores)


def pack_kernel(ids_ref, gates_ref, tokens_ref, out_ref, *, experts):
    count, width = tokens_ref.shape
    picks = ids_ref.shape[0]
    out_ref[:count, :] = tokens_ref[...]
    ids = ids_ref[...]
    gates = gates_ref[...].astype(jnp.float32)
    row = lax.broadcasted_iota(jnp.int32, (experts, count), 0)
    table = jnp.zeros((experts, count), jnp.float32)
    for k in range(picks):
        table += jnp.where(ids[k : k + 1, :] == row, gates[k : k + 1, :], 0.0)
    twice = jnp.concatenate([table, table], axis=1).astype(jnp.bfloat16)
    out_ref[count:, :] = jnp.zeros((SUB, width), jnp.bfloat16)
    for q in range(experts // SUB):
        out_ref[count:, q * LANES : (q + 1) * LANES] = twice[q * SUB : (q + 1) * SUB, :]


def pack(ids, gates, tokens, experts):
    count, width = tokens.shape
    return pl.pallas_call(
        functools.partial(pack_kernel, experts=experts),
        out_shape=jax.ShapeDtypeStruct((count + SUB, width), jnp.bfloat16),
        name="pack",
    )(ids.T, gates.T, tokens)


def one_hot(seat, cap):
    seats = lax.broadcasted_iota(jnp.int32, (cap, LANES), 0)
    return jnp.where(seats == seat, 1.0, 0.0)


def select_kernel(*refs, blocks, count, cap):
    where_ref = refs[0]
    block_refs = refs[1 : 1 + blocks]
    own_ref, other_ref, seat_ref, gate_ref = refs[1 + blocks : 5 + blocks]
    pairs = blocks // 2
    half = pairs // 2
    dot = functools.partial(jnp.dot, preferred_element_type=jnp.float32)
    tails = jnp.concatenate([r[count:, :] for r in block_refs], axis=0)
    upper = (
        lax.broadcasted_iota(jnp.int32, (LANES, LANES), 0)
        < lax.broadcasted_iota(jnp.int32, (LANES, LANES), 1)
    ).astype(jnp.bfloat16)
    left = lax.broadcasted_iota(jnp.int32, (pairs, pairs), 0)
    right = lax.broadcasted_iota(jnp.int32, (pairs, pairs), 1)
    before = ((right < left) & (right // half == left // half)).astype(jnp.bfloat16)
    lane = lax.broadcasted_iota(jnp.int32, (pairs, LANES), 1)
    row_of = lax.broadcasted_iota(jnp.int32, (pairs, blocks * SUB), 0)
    col_of = lax.broadcasted_iota(jnp.int32, (pairs, blocks * SUB), 1)
    groups = tails.shape[1] // LANES
    rows = [
        jnp.concatenate([r[:count, :] for r in block_refs[p * pairs : (p + 1) * pairs]], axis=0)
        for p in range(2)
    ]
    for k, out_ref in enumerate((own_ref, other_ref)):
        sub = where_ref[2 * k]
        group = where_ref[2 * k + 1]
        table = tails[:, :LANES]
        for q in range(1, groups):
            table = jnp.where(group == q, tails[:, q * LANES : (q + 1) * LANES], table)
        pick_a = (col_of == (2 * row_of) * SUB + sub).astype(jnp.bfloat16)
        pick_b = (col_of == (2 * row_of + 1) * SUB + sub).astype(jnp.bfloat16)
        gate = jnp.where(lane < count, dot(pick_a, table), dot(pick_b, table))
        chosen = gate > 0.0
        ones = jnp.where(chosen, 1.0, 0.0)
        total = jnp.broadcast_to(jnp.sum(ones, axis=1, keepdims=True), (pairs, LANES))
        spot = dot(ones.astype(jnp.bfloat16), upper) + dot(before, total.astype(jnp.bfloat16))
        spot = spot.astype(jnp.int32)
        seat = jnp.where(where_ref[4] == 0, spot, cap - 1 - spot)
        seat = jnp.where(chosen, seat, -1)
        seat_ref[k] = seat
        gate_ref[k] = gate
        for p in range(2):
            hot = jnp.concatenate(
                [one_hot(seat[o : o + 1, :], cap) for o in range(p * half, (p + 1) * half)], axis=1
            ).astype(jnp.bfloat16)
            out_ref[p * cap : (p + 1) * cap, :] = dot(hot, rows[p]).astype(jnp.bfloat16)


def select(where, blocks, count, cap):
    width = blocks[0].shape[1]
    pairs = len(blocks) // 2
    taken = jax.ShapeDtypeStruct((2 * cap, width), jnp.bfloat16)
    return pl.pallas_call(
        functools.partial(select_kernel, blocks=len(blocks), count=count, cap=cap),
        in_specs=[pl.BlockSpec(memory_space=pltpu.SMEM)]
        + [pl.BlockSpec(memory_space=pltpu.VMEM)] * len(blocks),
        out_shape=[
            taken,
            taken,
            jax.ShapeDtypeStruct((2, pairs, LANES), jnp.int32),
            jax.ShapeDtypeStruct((2, pairs, LANES), jnp.float32),
        ],
        name="select",
    )(where, *blocks)


def expert_kernel(own_ref, came_ref, w_in_ref, w_out_ref, out_ref, w_first, w_second, sem):
    first_copy = pltpu.make_async_copy(w_in_ref.at[0], w_first, sem.at[0])
    second_copy = pltpu.make_async_copy(w_out_ref.at[0], w_second, sem.at[1])
    first_copy.start()
    second_copy.start()
    rows = own_ref[...] + came_ref[...]
    first_copy.wait()
    hidden = jnp.dot(rows, w_first[...], preferred_element_type=jnp.float32)
    hidden = jnp.maximum(hidden, 0.0).astype(jnp.bfloat16)
    second_copy.wait()
    out_ref[...] = jnp.dot(hidden, w_second[...], preferred_element_type=jnp.float32).astype(
        jnp.bfloat16
    )


def expert(own, came, w_in, w_out):
    width, units = w_in.shape[1:]
    vmem = pl.BlockSpec(memory_space=pltpu.VMEM)
    anywhere = pl.BlockSpec(memory_space=pl.ANY)
    return pl.pallas_call(
        expert_kernel,
        in_specs=[vmem, vmem, anywhere, anywhere],
        out_shape=jax.ShapeDtypeStruct(own.shape, jnp.bfloat16),
        scratch_shapes=[
            pltpu.VMEM((width, units), jnp.bfloat16),
            pltpu.VMEM((units, width), jnp.bfloat16),
            pltpu.SemaphoreType.DMA((2,)),
        ],
        name="expert",
    )(own, came, w_in, w_out)


def spread_kernel(own_ref, came_ref, seat_ref, gate_ref, *out_refs, count, cap):
    pairs = seat_ref.shape[1]
    half = pairs // 2
    for p in range(2):
        value = None
        for k, ref in enumerate((own_ref, came_ref)):
            weights = jnp.concatenate(
                [
                    one_hot(seat_ref[k, o : o + 1, :], cap) * gate_ref[k, o : o + 1, :]
                    for o in range(p * half, (p + 1) * half)
                ],
                axis=1,
            ).astype(jnp.bfloat16)
            part = lax.dot_general(
                weights,
                ref[p * cap : (p + 1) * cap, :],
                (((0,), (0,)), ((), ())),
                preferred_element_type=jnp.float32,
            )
            value = part if value is None else value + part
        value = value.astype(jnp.bfloat16)
        for o in range(pairs):
            out_refs[p * pairs + o][...] = value[o * count : (o + 1) * count, :]


def spread(own, came, seat, gate, count, cap):
    blocks = 2 * seat.shape[1]
    out = jax.ShapeDtypeStruct((count, own.shape[1]), jnp.bfloat16)
    return pl.pallas_call(
        functools.partial(spread_kernel, count=count, cap=cap),
        out_shape=[out] * blocks,
        name="spread",
    )(own, came, seat, gate)


def on_rings(rings, tokens, expert_ids, gates, w_in, w_out):
    axes = ("grp", "dev")
    n_dev = lax.axis_size("dev")
    experts = lax.axis_size("grp") * n_dev
    count, width = tokens.shape
    length = rings.length
    if 2 * count != LANES or length % 4 or experts % SUB or experts * LANES > SUB * width:
        return per_device(tokens, expert_ids, gates, w_in, w_out)
    inverse = (rings.perms[1], rings.perms[0], rings.perms[2])
    where = np.asarray(
        [
            (here % SUB, here // SUB, mate % SUB, mate // SUB, core)
            for here, (mate, core) in enumerate(zip(rings.mates, rings.cores, strict=True))
        ],
        np.int32,
    )
    here = lax.axis_index("grp") * n_dev + lax.axis_index("dev")
    where = lax.dynamic_slice(jnp.asarray(where), (here, 0), (1, where.shape[1]))[0]

    held = {(0, 0): pack(expert_ids, gates, tokens, experts)}
    for chosen in rings.rounds:
        fresh = {}
        for channel, block in chosen.items():
            source = held[seen_from_source(channel, block, length)]
            fresh[block] = lax.ppermute(source, axes, rings.perms[channel])
        held.update(fresh)
    order = sorted(held, key=lambda b: (b[1], b[0]))
    cap = 4 * count
    own, other, seat, gate = select(where, [held[b] for b in order], count, cap)
    came = lax.ppermute(other, axes, rings.partner)
    result = expert(own, came, w_in, w_out)
    theirs = lax.ppermute(result, axes, rings.partner)
    sums = spread(result, theirs, seat, gate, count, cap)
    parts = {b: [sums[i]] for i, b in enumerate(order)}

    def total(block):
        value = parts[block][0].astype(jnp.float32)
        for more in parts[block][1:]:
            value = value + more.astype(jnp.float32)
        return value.astype(jnp.bfloat16)

    for chosen in reversed(rings.rounds):
        arrived = []
        for channel, block in chosen.items():
            value = lax.ppermute(total(block), axes, inverse[channel])
            arrived.append((seen_from_source(channel, block, length), value))
        for block, value in arrived:
            parts[block].append(value)
    return total((0, 0))


def earlier_count(onehot):
    return jnp.cumsum(onehot, axis=0) - onehot


def contract_rows(left, right):
    return lax.dot_general(
        left,
        right,
        (((0,), (0,)), ((), ())),
        precision=lax.Precision.HIGHEST,
        preferred_element_type=jnp.float32,
    )


def expert_rows(slot_block, w_first, w_second):

    def one_block(rows_block):
        hidden = jnp.maximum(
            jnp.dot(rows_block, w_first, preferred_element_type=jnp.float32), 0.0
        ).astype(jnp.bfloat16)
        return jnp.dot(hidden, w_second, preferred_element_type=jnp.float32).astype(jnp.bfloat16)

    return lax.map(one_block, slot_block)


def seat_sources(seat_of, valid, seat_total):
    item_count = seat_of.shape[0]
    target_seat = jnp.where(valid, seat_of, seat_total)
    empty_seats = jnp.full((seat_total,), item_count, jnp.int32)
    return empty_seats.at[target_seat].set(jnp.arange(item_count, dtype=jnp.int32), mode="drop")


def per_device(tokens, expert_ids, gates, w_in, w_out):
    n_grp = lax.axis_size("grp")
    n_dev = lax.axis_size("dev")
    token_count, feature_width = tokens.shape
    cap_grp = min(token_count, 3 * ((4 * token_count + n_grp - 1) // n_grp))
    cap_exp = min(4 * token_count, 24 * token_count // n_dev)
    seat_total = n_dev * cap_exp
    zero_half = jnp.zeros((), jnp.bfloat16)
    w_first = w_in[0]
    w_second = w_out[0]
    pair_ids = expert_ids.reshape(token_count * 4, 2)
    pair_group = pair_ids[:, 0] // n_dev
    group_hot = (pair_group[:, None] == jnp.arange(n_grp)[None, :]).astype(jnp.int32)
    group_rank = jnp.sum(earlier_count(group_hot) * group_hot, axis=1)
    target = pair_group * cap_grp + group_rank
    slot_count = n_grp * cap_grp
    placed = (target[None, :] == jnp.arange(slot_count)[:, None]).astype(jnp.int32)
    token_hot = placed.reshape(slot_count, token_count, 4).sum(axis=2)
    rows_out = jnp.dot(
        token_hot.astype(jnp.bfloat16), tokens, preferred_element_type=jnp.float32
    ).astype(jnp.bfloat16)
    local_ids = pair_ids % n_dev
    picks_out = jnp.dot(placed, local_ids + 1) - 1
    gains_out = jnp.dot(
        placed.astype(jnp.bfloat16),
        gates.reshape(token_count * 4, 2),
        preferred_element_type=jnp.float32,
    ).astype(jnp.bfloat16)
    rows_in, picks_in, gains_in = (
        lax.all_to_all(
            rows_out.reshape(n_grp, cap_grp, feature_width),
            "grp",
            split_axis=0,
            concat_axis=0,
            tiled=True,
        ),
        lax.all_to_all(
            picks_out.reshape(n_grp, cap_grp, 2), "grp", split_axis=0, concat_axis=0, tiled=True
        ),
        lax.all_to_all(
            gains_out.reshape(n_grp, cap_grp, 2), "grp", split_axis=0, concat_axis=0, tiled=True
        ),
    )
    relay_rows = rows_in.reshape(slot_count, feature_width)
    relay_picks = picks_in.reshape(slot_count, 2)
    relay_gains = gains_in.reshape(slot_count, 2)
    live_count = 4 * token_count
    slot_live = (relay_picks[:, 0] >= 0).astype(jnp.int32)
    slot_order = jnp.cumsum(slot_live) - 1
    packed = (
        (slot_order[None, :] == jnp.arange(live_count)[:, None]) & (slot_live[None, :] > 0)
    ).astype(jnp.int32)
    packed_rows = jnp.dot(
        packed.astype(jnp.bfloat16), relay_rows, preferred_element_type=jnp.float32
    ).astype(jnp.bfloat16)
    packed_picks = jnp.dot(packed, relay_picks)
    packed_gains = jnp.dot(
        packed.astype(jnp.bfloat16), relay_gains, preferred_element_type=jnp.float32
    ).astype(jnp.bfloat16)
    group_rows, group_picks, group_gains = (
        lax.all_gather(packed_rows, "dev", axis=0, tiled=True),
        lax.all_gather(packed_picks, "dev", axis=0, tiled=True),
        lax.all_gather(packed_gains, "dev", axis=0, tiled=True),
    )
    gathered_count = group_rows.shape[0]
    chosen = jnp.sum((group_picks == lax.axis_index("dev")).astype(jnp.int32), axis=1)
    expert_seat = jnp.cumsum(chosen) - 1
    seat_source = seat_sources(expert_seat, chosen > 0, seat_total)
    seat_live = seat_source < gathered_count
    taken_rows = jnp.take(group_rows, jnp.minimum(seat_source, gathered_count - 1), axis=0)
    expert_in = jnp.where(seat_live[:, None], taken_rows, zero_half)
    expert_out = expert_rows(
        expert_in.reshape(n_dev, cap_exp, feature_width), w_first, w_second
    ).reshape(seat_total, feature_width)
    spread_rows = jnp.take(expert_out, jnp.clip(expert_seat, 0, seat_total - 1), axis=0)
    spread = jnp.where((chosen > 0)[:, None], spread_rows, zero_half)
    back = lax.all_to_all(
        spread.reshape(n_dev, live_count, feature_width),
        "dev",
        split_axis=0,
        concat_axis=0,
        tiled=True,
    )
    match = (packed_picks[None, :, :] == jnp.arange(n_dev)[:, None, None]).astype(jnp.float32)
    row_weights = jnp.sum(match * packed_gains.astype(jnp.float32)[None, :, :], axis=2)
    packed_sum = jnp.sum(row_weights[:, :, None] * back.astype(jnp.float32), axis=0)
    partial_value = contract_rows(packed.astype(jnp.float32), packed_sum)
    returned_sums = lax.all_to_all(
        partial_value.reshape(n_grp, cap_grp, feature_width),
        "grp",
        split_axis=0,
        concat_axis=0,
        tiled=True,
    )
    mixed = contract_rows(
        token_hot.astype(jnp.float32), returned_sums.reshape(slot_count, feature_width)
    )
    return mixed.astype(jnp.bfloat16)


def solution(mesh):
    rings = find_rings(mesh)
    body = per_device if rings is None else functools.partial(on_rings, rings)
    return jax.shard_map(
        body,
        mesh=mesh,
        in_specs=(
            P(("grp", "dev"), None),
            P(("grp", "dev"), None),
            P(("grp", "dev"), None),
            P(("grp", "dev"), None, None),
            P(("grp", "dev"), None, None),
        ),
        out_specs=P(("grp", "dev"), None),
        check_vma=False,
    )
```

```python
import functools

import jax
import jax.numpy as jnp
import numpy as np
from jax import lax
from jax.experimental import pallas as pl
from jax.experimental.pallas import tpu as pltpu
from jax.sharding import PartitionSpec as P

LANES = 128
SUB = 8
MIB = 1 << 20


class Rings:
    def __init__(self, length, rounds, clockwise, counter, mirror, partner, cores):
        self.length = length
        self.rounds = rounds
        self.perms = (clockwise, counter, mirror)
        self.partner = partner
        self.mates = [mate for _, mate in sorted(partner)]
        self.cores = cores


def wrap(step, length):
    step %= length
    return step - length if step > length // 2 else step


def seen_from_source(channel, block, length):
    step, plane = block
    if channel == 0:
        return (wrap(step + 1, length), plane)
    if channel == 1:
        return (wrap(step - 1, length), plane)
    return (step, 1 - plane)


def gather_rounds(length):
    everything = [(wrap(s, length), p) for p in range(2) for s in range(length)]
    everything.sort(key=lambda b: (b[1], abs(b[0]), -b[0]))
    held = {(0, 0)}
    rounds = []
    while len(held) < len(everything):
        chosen = {}
        for channel in range(3):
            for block in everything:
                if block in held or block in chosen.values():
                    continue
                if channel == 2 and block[1] == 0:
                    continue
                if seen_from_source(channel, block, length) in held:
                    chosen[channel] = block
                    break
        rounds.append(chosen)
        held |= set(chosen.values())
    return rounds


def find_rings(mesh):
    grid = mesh.devices
    n_grp, n_dev = grid.shape
    if n_dev != 2 or not hasattr(grid[0, 0], "coords"):
        return None
    place = {}
    for g in range(n_grp):
        for d in range(n_dev):
            device = grid[g, d]
            place[(tuple(device.coords), device.core_on_chip)] = (g, d)
    planes = []
    for d in range(n_dev):
        planes.append(sorted({tuple(grid[g, d].coords) for g in range(n_grp)}))
    if 2 * len(planes[0]) != n_grp or set(planes[0]) & set(planes[1]):
        return None
    wide = [a for a in range(3) if len({c[a] for c in planes[0]}) == 2]
    flat = [a for a in range(3) if len({c[a] for c in planes[0]}) == 1]
    if not wide or len(flat) != 1:
        return None
    side = wide[0]
    along = [a for a in range(3) if a not in (side, flat[0])][0]
    low = min(c[side] for c in planes[0])
    up = sorted((c for c in planes[0] if c[side] == low), key=lambda c: c[along])
    down = sorted((c for c in planes[0] if c[side] != low), key=lambda c: -c[along])
    order = up + down
    length = len(order)

    def index(chip, core):
        g, d = place[(chip, core)]
        return g * n_dev + d

    def mirrored(chip):
        other = planes[1][0][flat[0]]
        return tuple(other if a == flat[0] else v for a, v in enumerate(chip))

    if any((mirrored(c), k) not in place or (c, k) not in place for c in order for k in range(2)):
        return None
    if any(place[(c, k)][0] != place[(mirrored(c), k)][0] for c in order for k in range(2)):
        return None
    clockwise, counter, mirror, partner = [], [], [], []
    for here in range(length):
        after = (here + 1) % length
        for core in range(2):
            for turn in (lambda c: c, mirrored):
                a, b = index(turn(order[here]), core), index(turn(order[after]), core)
                clockwise.append((a, b))
                counter.append((b, a))
                partner.append((a, index(turn(order[here]), 1 - core)))
            a, b = index(order[here], core), index(mirrored(order[here]), core)
            mirror += [(a, b), (b, a)]
    cores = [device.core_on_chip for device in grid.flat]
    return Rings(length, gather_rounds(length), clockwise, counter, mirror, partner, cores)


def pack_kernel(ids_ref, gates_ref, tokens_ref, out_ref, *, experts):
    count, width = tokens_ref.shape
    picks = ids_ref.shape[0]
    out_ref[:count, :] = tokens_ref[...]
    ids = ids_ref[...]
    gates = gates_ref[...].astype(jnp.float32)
    row = lax.broadcasted_iota(jnp.int32, (experts, count), 0)
    table = jnp.zeros((experts, count), jnp.float32)
    for k in range(picks):
        table += jnp.where(ids[k : k + 1, :] == row, gates[k : k + 1, :], 0.0)
    twice = jnp.concatenate([table, table], axis=1).astype(jnp.bfloat16)
    out_ref[count:, :] = jnp.zeros((SUB, width), jnp.bfloat16)
    for q in range(experts // SUB):
        out_ref[count:, q * LANES : (q + 1) * LANES] = twice[q * SUB : (q + 1) * SUB, :]


def pack(ids, gates, tokens, experts):
    count, width = tokens.shape
    return pl.pallas_call(
        functools.partial(pack_kernel, experts=experts),
        out_shape=jax.ShapeDtypeStruct((count + SUB, width), jnp.bfloat16),
        name="pack",
        compiler_params=pltpu.CompilerParams(vmem_limit_bytes=2 * MIB),
    )(ids.T, gates.T, tokens)


def one_hot(seat, cap):
    seats = lax.broadcasted_iota(jnp.int32, (cap, LANES), 0)
    return jnp.where(seats == seat, 1.0, 0.0)


def select_kernel(*refs, blocks, count, cap):
    where_ref = refs[0]
    block_refs = refs[1 : 1 + blocks]
    own_ref, other_ref, seat_ref, gate_ref = refs[1 + blocks : 5 + blocks]
    pairs = blocks // 2
    half = pairs // 2
    dot = functools.partial(jnp.dot, preferred_element_type=jnp.float32)
    tails = jnp.concatenate([r[count:, :] for r in block_refs], axis=0)
    upper = (
        lax.broadcasted_iota(jnp.int32, (LANES, LANES), 0)
        < lax.broadcasted_iota(jnp.int32, (LANES, LANES), 1)
    ).astype(jnp.bfloat16)
    left = lax.broadcasted_iota(jnp.int32, (pairs, pairs), 0)
    right = lax.broadcasted_iota(jnp.int32, (pairs, pairs), 1)
    before = ((right < left) & (right // half == left // half)).astype(jnp.bfloat16)
    lane = lax.broadcasted_iota(jnp.int32, (pairs, LANES), 1)
    row_of = lax.broadcasted_iota(jnp.int32, (pairs, blocks * SUB), 0)
    col_of = lax.broadcasted_iota(jnp.int32, (pairs, blocks * SUB), 1)
    groups = tails.shape[1] // LANES
    rows = [
        jnp.concatenate([r[:count, :] for r in block_refs[p * pairs : (p + 1) * pairs]], axis=0)
        for p in range(2)
    ]
    for k, out_ref in enumerate((own_ref, other_ref)):
        sub = where_ref[2 * k]
        group = where_ref[2 * k + 1]
        table = tails[:, :LANES]
        for q in range(1, groups):
            table = jnp.where(group == q, tails[:, q * LANES : (q + 1) * LANES], table)
        pick_a = (col_of == (2 * row_of) * SUB + sub).astype(jnp.bfloat16)
        pick_b = (col_of == (2 * row_of + 1) * SUB + sub).astype(jnp.bfloat16)
        gate = jnp.where(lane < count, dot(pick_a, table), dot(pick_b, table))
        chosen = gate > 0.0
        ones = jnp.where(chosen, 1.0, 0.0)
        total = jnp.broadcast_to(jnp.sum(ones, axis=1, keepdims=True), (pairs, LANES))
        spot = dot(ones.astype(jnp.bfloat16), upper) + dot(before, total.astype(jnp.bfloat16))
        spot = spot.astype(jnp.int32)
        seat = jnp.where(where_ref[4] == 0, spot, cap - 1 - spot)
        seat = jnp.where(chosen, seat, -1)
        seat_ref[k] = seat
        gate_ref[k] = gate
        for p in range(2):
            hot = jnp.concatenate(
                [one_hot(seat[o : o + 1, :], cap) for o in range(p * half, (p + 1) * half)], axis=1
            ).astype(jnp.bfloat16)
            out_ref[p * cap : (p + 1) * cap, :] = dot(hot, rows[p]).astype(jnp.bfloat16)


def select(where, blocks, count, cap):
    width = blocks[0].shape[1]
    pairs = len(blocks) // 2
    taken = jax.ShapeDtypeStruct((2 * cap, width), jnp.bfloat16)
    return pl.pallas_call(
        functools.partial(select_kernel, blocks=len(blocks), count=count, cap=cap),
        in_specs=[pl.BlockSpec(memory_space=pltpu.SMEM)]
        + [pl.BlockSpec(memory_space=pltpu.VMEM)] * len(blocks),
        out_shape=[
            taken,
            taken,
            jax.ShapeDtypeStruct((2, pairs, LANES), jnp.int32),
            jax.ShapeDtypeStruct((2, pairs, LANES), jnp.float32),
        ],
        name="select",
        compiler_params=pltpu.CompilerParams(vmem_limit_bytes=20 * MIB),
    )(where, *blocks)


def expert_kernel(own_ref, came_ref, w_in_ref, w_out_ref, out_ref):
    rows = own_ref[...] + came_ref[...]
    hidden = jnp.dot(rows, w_in_ref[0], preferred_element_type=jnp.float32)
    hidden = jnp.maximum(hidden, 0.0).astype(jnp.bfloat16)
    result = jnp.dot(hidden, w_out_ref[0], preferred_element_type=jnp.float32)
    out_ref[...] = result.astype(jnp.bfloat16)


def expert(own, came, w_in, w_out):
    vmem = pl.BlockSpec(memory_space=pltpu.VMEM)
    return pl.pallas_call(
        expert_kernel,
        in_specs=[vmem] * 4,
        out_shape=jax.ShapeDtypeStruct(own.shape, jnp.bfloat16),
        name="expert",
        compiler_params=pltpu.CompilerParams(vmem_limit_bytes=20 * MIB),
    )(own, came, w_in, w_out)


def spread_kernel(own_ref, came_ref, seat_ref, gate_ref, *out_refs, count, cap):
    pairs = seat_ref.shape[1]
    half = pairs // 2
    for p in range(2):
        value = None
        for k, ref in enumerate((own_ref, came_ref)):
            weights = jnp.concatenate(
                [
                    one_hot(seat_ref[k, o : o + 1, :], cap) * gate_ref[k, o : o + 1, :]
                    for o in range(p * half, (p + 1) * half)
                ],
                axis=1,
            ).astype(jnp.bfloat16)
            part = lax.dot_general(
                weights,
                ref[p * cap : (p + 1) * cap, :],
                (((0,), (0,)), ((), ())),
                preferred_element_type=jnp.float32,
            )
            value = part if value is None else value + part
        value = value.astype(jnp.bfloat16)
        for o in range(pairs):
            out_refs[p * pairs + o][...] = value[o * count : (o + 1) * count, :]


def spread(own, came, seat, gate, count, cap):
    blocks = 2 * seat.shape[1]
    out = jax.ShapeDtypeStruct((count, own.shape[1]), jnp.bfloat16)
    return pl.pallas_call(
        functools.partial(spread_kernel, count=count, cap=cap),
        out_shape=[out] * blocks,
        name="spread",
        compiler_params=pltpu.CompilerParams(vmem_limit_bytes=20 * MIB),
    )(own, came, seat, gate)


def on_rings(rings, tokens, expert_ids, gates, w_in, w_out):
    axes = ("grp", "dev")
    n_dev = lax.axis_size("dev")
    experts = lax.axis_size("grp") * n_dev
    count, width = tokens.shape
    length = rings.length
    if 2 * count != LANES or length % 4 or experts % SUB or experts * LANES > SUB * width:
        return per_device(tokens, expert_ids, gates, w_in, w_out)
    inverse = (rings.perms[1], rings.perms[0], rings.perms[2])
    where = np.asarray(
        [
            (here % SUB, here // SUB, mate % SUB, mate // SUB, core)
            for here, (mate, core) in enumerate(zip(rings.mates, rings.cores, strict=True))
        ],
        np.int32,
    )
    here = lax.axis_index("grp") * n_dev + lax.axis_index("dev")
    where = lax.dynamic_slice(jnp.asarray(where), (here, 0), (1, where.shape[1]))[0]

    held = {(0, 0): pack(expert_ids, gates, tokens, experts)}
    for chosen in rings.rounds:
        fresh = {}
        for channel, block in chosen.items():
            source = held[seen_from_source(channel, block, length)]
            fresh[block] = lax.ppermute(source, axes, rings.perms[channel])
        held.update(fresh)
    order = sorted(held, key=lambda b: (b[1], b[0]))
    cap = 4 * count
    own, other, seat, gate = select(where, [held[b] for b in order], count, cap)
    came = lax.ppermute(other, axes, rings.partner)
    result = expert(own, came, w_in, w_out)
    theirs = lax.ppermute(result, axes, rings.partner)
    sums = spread(result, theirs, seat, gate, count, cap)
    parts = {b: [sums[i]] for i, b in enumerate(order)}

    def total(block):
        value = parts[block][0].astype(jnp.float32)
        for more in parts[block][1:]:
            value = value + more.astype(jnp.float32)
        return value.astype(jnp.bfloat16)

    for chosen in reversed(rings.rounds):
        arrived = []
        for channel, block in chosen.items():
            value = lax.ppermute(total(block), axes, inverse[channel])
            arrived.append((seen_from_source(channel, block, length), value))
        for block, value in arrived:
            parts[block].append(value)
    return total((0, 0))


def earlier_count(onehot):
    return jnp.cumsum(onehot, axis=0) - onehot


def contract_rows(left, right):
    return lax.dot_general(
        left,
        right,
        (((0,), (0,)), ((), ())),
        precision=lax.Precision.HIGHEST,
        preferred_element_type=jnp.float32,
    )


def expert_rows(slot_block, w_first, w_second):

    def one_block(rows_block):
        hidden = jnp.maximum(
            jnp.dot(rows_block, w_first, preferred_element_type=jnp.float32), 0.0
        ).astype(jnp.bfloat16)
        return jnp.dot(hidden, w_second, preferred_element_type=jnp.float32).astype(jnp.bfloat16)

    return lax.map(one_block, slot_block)


def seat_sources(seat_of, valid, seat_total):
    item_count = seat_of.shape[0]
    target_seat = jnp.where(valid, seat_of, seat_total)
    empty_seats = jnp.full((seat_total,), item_count, jnp.int32)
    return empty_seats.at[target_seat].set(jnp.arange(item_count, dtype=jnp.int32), mode="drop")


def per_device(tokens, expert_ids, gates, w_in, w_out):
    n_grp = lax.axis_size("grp")
    n_dev = lax.axis_size("dev")
    token_count, feature_width = tokens.shape
    cap_grp = min(token_count, 3 * ((4 * token_count + n_grp - 1) // n_grp))
    cap_exp = min(4 * token_count, 24 * token_count // n_dev)
    seat_total = n_dev * cap_exp
    zero_half = jnp.zeros((), jnp.bfloat16)
    w_first = w_in[0]
    w_second = w_out[0]
    pair_ids = expert_ids.reshape(token_count * 4, 2)
    pair_group = pair_ids[:, 0] // n_dev
    group_hot = (pair_group[:, None] == jnp.arange(n_grp)[None, :]).astype(jnp.int32)
    group_rank = jnp.sum(earlier_count(group_hot) * group_hot, axis=1)
    target = pair_group * cap_grp + group_rank
    slot_count = n_grp * cap_grp
    placed = (target[None, :] == jnp.arange(slot_count)[:, None]).astype(jnp.int32)
    token_hot = placed.reshape(slot_count, token_count, 4).sum(axis=2)
    rows_out = jnp.dot(
        token_hot.astype(jnp.bfloat16), tokens, preferred_element_type=jnp.float32
    ).astype(jnp.bfloat16)
    local_ids = pair_ids % n_dev
    picks_out = jnp.dot(placed, local_ids + 1) - 1
    gains_out = jnp.dot(
        placed.astype(jnp.bfloat16),
        gates.reshape(token_count * 4, 2),
        preferred_element_type=jnp.float32,
    ).astype(jnp.bfloat16)
    rows_in, picks_in, gains_in = (
        lax.all_to_all(
            rows_out.reshape(n_grp, cap_grp, feature_width),
            "grp",
            split_axis=0,
            concat_axis=0,
            tiled=True,
        ),
        lax.all_to_all(
            picks_out.reshape(n_grp, cap_grp, 2), "grp", split_axis=0, concat_axis=0, tiled=True
        ),
        lax.all_to_all(
            gains_out.reshape(n_grp, cap_grp, 2), "grp", split_axis=0, concat_axis=0, tiled=True
        ),
    )
    relay_rows = rows_in.reshape(slot_count, feature_width)
    relay_picks = picks_in.reshape(slot_count, 2)
    relay_gains = gains_in.reshape(slot_count, 2)
    live_count = 4 * token_count
    slot_live = (relay_picks[:, 0] >= 0).astype(jnp.int32)
    slot_order = jnp.cumsum(slot_live) - 1
    packed = (
        (slot_order[None, :] == jnp.arange(live_count)[:, None]) & (slot_live[None, :] > 0)
    ).astype(jnp.int32)
    packed_rows = jnp.dot(
        packed.astype(jnp.bfloat16), relay_rows, preferred_element_type=jnp.float32
    ).astype(jnp.bfloat16)
    packed_picks = jnp.dot(packed, relay_picks)
    packed_gains = jnp.dot(
        packed.astype(jnp.bfloat16), relay_gains, preferred_element_type=jnp.float32
    ).astype(jnp.bfloat16)
    group_rows, group_picks, group_gains = (
        lax.all_gather(packed_rows, "dev", axis=0, tiled=True),
        lax.all_gather(packed_picks, "dev", axis=0, tiled=True),
        lax.all_gather(packed_gains, "dev", axis=0, tiled=True),
    )
    gathered_count = group_rows.shape[0]
    chosen = jnp.sum((group_picks == lax.axis_index("dev")).astype(jnp.int32), axis=1)
    expert_seat = jnp.cumsum(chosen) - 1
    seat_source = seat_sources(expert_seat, chosen > 0, seat_total)
    seat_live = seat_source < gathered_count
    taken_rows = jnp.take(group_rows, jnp.minimum(seat_source, gathered_count - 1), axis=0)
    expert_in = jnp.where(seat_live[:, None], taken_rows, zero_half)
    expert_out = expert_rows(
        expert_in.reshape(n_dev, cap_exp, feature_width), w_first, w_second
    ).reshape(seat_total, feature_width)
    spread_rows = jnp.take(expert_out, jnp.clip(expert_seat, 0, seat_total - 1), axis=0)
    spread = jnp.where((chosen > 0)[:, None], spread_rows, zero_half)
    back = lax.all_to_all(
        spread.reshape(n_dev, live_count, feature_width),
        "dev",
        split_axis=0,
        concat_axis=0,
        tiled=True,
    )
    match = (packed_picks[None, :, :] == jnp.arange(n_dev)[:, None, None]).astype(jnp.float32)
    row_weights = jnp.sum(match * packed_gains.astype(jnp.float32)[None, :, :], axis=2)
    packed_sum = jnp.sum(row_weights[:, :, None] * back.astype(jnp.float32), axis=0)
    partial_value = contract_rows(packed.astype(jnp.float32), packed_sum)
    returned_sums = lax.all_to_all(
        partial_value.reshape(n_grp, cap_grp, feature_width),
        "grp",
        split_axis=0,
        concat_axis=0,
        tiled=True,
    )
    mixed = contract_rows(
        token_hot.astype(jnp.float32), returned_sums.reshape(slot_count, feature_width)
    )
    return mixed.astype(jnp.bfloat16)


def solution(mesh):
    rings = find_rings(mesh)
    body = per_device if rings is None else functools.partial(on_rings, rings)
    return jax.shard_map(
        body,
        mesh=mesh,
        in_specs=(
            P(("grp", "dev"), None),
            P(("grp", "dev"), None),
            P(("grp", "dev"), None),
            P(("grp", "dev"), None, None),
            P(("grp", "dev"), None, None),
        ),
        out_specs=P(("grp", "dev"), None),
        check_vma=False,
    )
```

```python
import functools

import jax
import jax.numpy as jnp
from jax import lax
from jax.experimental import pallas as pl
from jax.experimental.pallas import tpu as pltpu
from jax.sharding import PartitionSpec as P


LANES = 128
SUB = 8
MIB = 1 << 20


class Rings:
    def __init__(self, length, clockwise, counter, mirror, partner):
        self.length = length
        self.perms = (clockwise, counter, mirror)
        self.partner = partner


def wrap(step, length):
    step %= length
    return step - length if step > length // 2 else step


def seen_from_source(channel, block, length):
    step, plane = block
    if channel == 0:
        return (wrap(step + 1, length), plane)
    if channel == 1:
        return (wrap(step - 1, length), plane)
    return (step, 1 - plane)


def gather_sequence():
    return (
        (0, (-1, 0)),
        (1, (1, 0)),
        (2, (0, 1)),
        (0, (-2, 0)),
        (1, (2, 0)),
        (2, (1, 1)),
        (0, (-3, 0)),
        (1, (3, 0)),
        (2, (-2, 1)),
        (0, (4, 0)),
        (1, (2, 1)),
        (2, (-1, 1)),
        (0, (-3, 1)),
        (1, (3, 1)),
        (2, (4, 1)),
    )


def return_sequence():
    return (
        (2, (4, 1)),
        (0, (-3, 1)),
        (1, (3, 1)),
        (2, (-1, 1)),
        (0, (4, 0)),
        (1, (2, 1)),
        (2, (-2, 1)),
        (0, (-3, 0)),
        (1, (3, 0)),
        (2, (1, 1)),
        (0, (-2, 0)),
        (1, (2, 0)),
        (2, (0, 1)),
        (0, (-1, 0)),
        (1, (1, 0)),
    )


def find_rings(mesh):
    grid = mesh.devices
    n_grp, n_dev = grid.shape
    if n_dev != 2 or not hasattr(grid[0, 0], "coords"):
        return None
    place = {}
    for g in range(n_grp):
        for d in range(n_dev):
            device = grid[g, d]
            place[(tuple(device.coords), device.core_on_chip)] = (g, d)
    planes = []
    for d in range(n_dev):
        planes.append(sorted({tuple(grid[g, d].coords) for g in range(n_grp)}))
    if 2 * len(planes[0]) != n_grp or set(planes[0]) & set(planes[1]):
        return None
    wide = [a for a in range(3) if len({c[a] for c in planes[0]}) == 2]
    flat = [a for a in range(3) if len({c[a] for c in planes[0]}) == 1]
    if not wide or len(flat) != 1:
        return None
    side = wide[0]
    along = [a for a in range(3) if a not in (side, flat[0])][0]
    low = min(c[side] for c in planes[0])
    up = sorted((c for c in planes[0] if c[side] == low), key=lambda c: c[along])
    down = sorted((c for c in planes[0] if c[side] != low), key=lambda c: -c[along])
    order = up + down
    length = len(order)
    if length != 8:
        return None

    def index(chip, core):
        g, d = place[(chip, core)]
        return g * n_dev + d

    def mirrored(chip):
        other = planes[1][0][flat[0]]
        return tuple(other if a == flat[0] else v for a, v in enumerate(chip))

    if any((mirrored(c), k) not in place or (c, k) not in place for c in order for k in range(2)):
        return None
    if any(place[(c, k)][0] != place[(mirrored(c), k)][0] for c in order for k in range(2)):
        return None
    clockwise, counter, mirror, partner = [], [], [], []
    for here in range(length):
        after = (here + 1) % length
        for core in range(2):
            for turn in (lambda c: c, mirrored):
                a, b = index(turn(order[here]), core), index(turn(order[after]), core)
                clockwise.append((a, b))
                counter.append((b, a))
                partner.append((a, index(turn(order[here]), 1 - core)))
            a, b = index(order[here], core), index(mirrored(order[here]), core)
            mirror += [(a, b), (b, a)]
    if any(mate != one ^ n_dev for one, mate in partner):
        return None
    return Rings(length, clockwise, counter, mirror, partner)


def pack_kernel(ids_hbm, gates_hbm, tokens_hbm, out_ref, ids_ref, gates_ref, sem, *, experts):
    count, width = tokens_hbm.shape
    picks = ids_ref.shape[0]
    copies = [
        pltpu.make_async_copy(tokens_hbm, out_ref.at[pl.ds(0, count)], sem.at[0]),
        pltpu.make_async_copy(ids_hbm, ids_ref, sem.at[1]),
        pltpu.make_async_copy(gates_hbm, gates_ref, sem.at[2]),
    ]
    for copy in copies:
        copy.start()
    row = lax.broadcasted_iota(jnp.int32, (experts, count), 0)
    table = jnp.zeros((experts, count), jnp.float32)
    copies[1].wait()
    copies[2].wait()
    ids = ids_ref[...]
    gates = gates_ref[...].astype(jnp.float32)
    for k in range(picks):
        table += jnp.where(ids[k : k + 1, :] == row, gates[k : k + 1, :], 0.0)
    twice = jnp.concatenate([table, table], axis=1).astype(jnp.bfloat16)
    out_ref[count:, :] = jnp.zeros((SUB, width), jnp.bfloat16)
    for q in range(experts // SUB):
        out_ref[count:, q * LANES : (q + 1) * LANES] = twice[q * SUB : (q + 1) * SUB, :]
    copies[0].wait()


def pack(ids, gates, tokens, experts):
    count, width = tokens.shape
    picks = ids.shape[1]
    return pl.pallas_call(
        functools.partial(pack_kernel, experts=experts),
        in_specs=[pl.BlockSpec(memory_space=pltpu.HBM)] * 3,
        out_shape=jax.ShapeDtypeStruct((count + SUB, width), jnp.bfloat16),
        scratch_shapes=[
            pltpu.VMEM((picks, count), jnp.int32),
            pltpu.VMEM((picks, count), jnp.bfloat16),
            pltpu.SemaphoreType.DMA((3,)),
        ],
        name="pack",
        compiler_params=pltpu.CompilerParams(vmem_limit_bytes=2 * MIB),
    )(*(pltpu.with_memory_space_constraint(x, pltpu.HBM) for x in (ids.T, gates.T, tokens)))


def one_hot(seat, cap):
    seats = lax.broadcasted_iota(jnp.int32, (cap, LANES), 0)
    return jnp.where(seats == seat, 1.0, 0.0)


def select_kernel(*refs, blocks, count, cap, stride):
    here = lax.axis_index("grp") * stride + lax.axis_index("dev")
    mate = here ^ stride
    block_refs = refs[:blocks]
    own_ref, other_ref, seat_ref, gate_ref = refs[-4:]
    pairs = blocks // 2
    dot = functools.partial(jnp.dot, preferred_element_type=jnp.float32)
    tails = jnp.concatenate([r[count:, :] for r in block_refs], axis=0)
    upper = (
        lax.broadcasted_iota(jnp.int32, (LANES, LANES), 0)
        < lax.broadcasted_iota(jnp.int32, (LANES, LANES), 1)
    ).astype(jnp.bfloat16)
    before = (
        lax.broadcasted_iota(jnp.int32, (pairs, pairs), 1)
        < lax.broadcasted_iota(jnp.int32, (pairs, pairs), 0)
    ).astype(jnp.bfloat16)
    lane = lax.broadcasted_iota(jnp.int32, (pairs, LANES), 1)
    row_of = lax.broadcasted_iota(jnp.int32, (pairs, blocks * SUB), 0)
    col_of = lax.broadcasted_iota(jnp.int32, (pairs, blocks * SUB), 1)
    groups = tails.shape[1] // LANES
    rows = jnp.concatenate([r[:count, :] for r in block_refs], axis=0)
    for k, out_ref in enumerate((own_ref, other_ref)):
        expert = (here, mate)[k]
        sub = expert % SUB
        group = expert // SUB
        table = tails[:, :LANES]
        for q in range(1, groups):
            table = jnp.where(group == q, tails[:, q * LANES : (q + 1) * LANES], table)
        pick_a = (col_of == (2 * row_of) * SUB + sub).astype(jnp.bfloat16)
        pick_b = (col_of == (2 * row_of + 1) * SUB + sub).astype(jnp.bfloat16)
        gate = jnp.where(lane < count, dot(pick_a, table), dot(pick_b, table))
        chosen = gate > 0.0
        ones = jnp.where(chosen, 1.0, 0.0)
        inside = dot(ones.astype(jnp.bfloat16), upper)
        total = jnp.broadcast_to(jnp.sum(ones, axis=1, keepdims=True), (pairs, LANES))
        spot = (inside + dot(before, total.astype(jnp.bfloat16))).astype(jnp.int32)
        seat = jnp.where(here < mate, spot, cap - 1 - spot)
        seat = jnp.where(chosen, seat, -1)
        seat_ref[k] = seat
        gate_ref[k] = gate
        hot = jnp.concatenate([one_hot(seat[o : o + 1, :], cap) for o in range(pairs)], axis=1)
        out_ref[...] = dot(hot.astype(jnp.bfloat16), rows).astype(jnp.bfloat16)


def select(blocks, count, cap, stride):
    width = blocks[0].shape[1]
    pairs = len(blocks) // 2
    taken = jax.ShapeDtypeStruct((cap, width), jnp.bfloat16)
    vmem = pl.BlockSpec(memory_space=pltpu.VMEM)
    return pl.pallas_call(
        functools.partial(select_kernel, blocks=len(blocks), count=count, cap=cap, stride=stride),
        in_specs=[vmem] * len(blocks),
        out_shape=[
            taken,
            taken,
            jax.ShapeDtypeStruct((2, pairs, LANES), jnp.int32),
            jax.ShapeDtypeStruct((2, pairs, LANES), jnp.float32),
        ],
        name="select",
        compiler_params=pltpu.CompilerParams(vmem_limit_bytes=16 * MIB),
    )(*blocks)


def load_kernel(source, out_ref, sems, *, at):
    pieces = sems.shape[0]
    rows = out_ref.shape[0] // pieces
    copies = [
        pltpu.make_async_copy(
            source.at[0, pl.ds(at[0] + p * rows, rows), pl.ds(at[1], out_ref.shape[1])],
            out_ref.at[pl.ds(p * rows, rows)],
            sems.at[p],
        )
        for p in range(pieces)
    ]
    for copy in copies:
        copy.start()
    for copy in copies:
        copy.wait()


def load(weights, at, shape):
    return pl.pallas_call(
        functools.partial(load_kernel, at=at),
        in_specs=[pl.BlockSpec(memory_space=pltpu.HBM)],
        out_shape=jax.ShapeDtypeStruct(shape, weights.dtype),
        scratch_shapes=[pltpu.SemaphoreType.DMA((8,))],
        name="load",
        compiler_params=pltpu.CompilerParams(vmem_limit_bytes=4 * MIB),
    )(pltpu.with_memory_space_constraint(weights, pltpu.HBM))


def expert_kernel(own_ref, came_ref, in_a, in_b, out_a, out_b, out_ref):
    dot = functools.partial(jnp.dot, preferred_element_type=jnp.float32)
    rows = own_ref[...] + came_ref[...]
    result = None
    for first, second in ((in_a, out_a), (in_b, out_b)):
        hidden = jnp.maximum(dot(rows, first[...]), 0.0).astype(jnp.bfloat16)
        part = dot(hidden, second[...])
        result = part if result is None else result + part
    out_ref[...] = result.astype(jnp.bfloat16)


def expert(own, came, weights):
    vmem = pl.BlockSpec(memory_space=pltpu.VMEM)
    return pl.pallas_call(
        expert_kernel,
        in_specs=[vmem] * (2 + len(weights)),
        out_shape=jax.ShapeDtypeStruct(own.shape, jnp.bfloat16),
        name="expert",
        compiler_params=pltpu.CompilerParams(vmem_limit_bytes=16 * MIB),
    )(own, came, *weights)


def spread_kernel(own_ref, came_ref, seat_ref, gate_ref, *out_refs, count, cap):
    pairs = seat_ref.shape[1]
    value = None
    for k, ref in enumerate((own_ref, came_ref)):
        weights = jnp.concatenate(
            [
                one_hot(seat_ref[k, o : o + 1, :], cap) * gate_ref[k, o : o + 1, :]
                for o in range(pairs)
            ],
            axis=1,
        ).astype(jnp.bfloat16)
        part = lax.dot_general(
            weights, ref[...], (((0,), (0,)), ((), ())), preferred_element_type=jnp.float32
        )
        value = part if value is None else value + part
    value = value.astype(jnp.bfloat16)
    for o, out_ref in enumerate(out_refs):
        out_ref[...] = value[o * count : (o + 1) * count, :]


def spread(own, came, seat, gate, count):
    blocks = 2 * seat.shape[1]
    cap, width = own.shape
    out = jax.ShapeDtypeStruct((count, width), jnp.bfloat16)
    return pl.pallas_call(
        functools.partial(spread_kernel, count=count, cap=cap),
        out_shape=[out] * blocks,
        name="spread",
        compiler_params=pltpu.CompilerParams(vmem_limit_bytes=12 * MIB),
    )(own, came, seat, gate)


def on_rings(rings, tokens, expert_ids, gates, w_in, w_out):
    axes = ("grp", "dev")
    n_dev = lax.axis_size("dev")
    experts = lax.axis_size("grp") * n_dev
    count, width = tokens.shape
    length = rings.length
    if 2 * count != LANES or length % 4 or experts % SUB or experts * LANES > SUB * width:
        return per_device(tokens, expert_ids, gates, w_in, w_out)
    inverse = (rings.perms[1], rings.perms[0], rings.perms[2])
    held = {(0, 0): pack(expert_ids, gates, tokens, experts)}
    for channel, block in gather_sequence():
        source = held[seen_from_source(channel, block, length)]
        held[block] = lax.ppermute(source, axes, rings.perms[channel])
    order = sorted(held, key=lambda b: (b[1], b[0]))
    cap = 4 * count
    units = w_in.shape[2]
    weights = []
    for array, at, shape in (
        (w_in, (0, 0), (width, units // 2)),
        (w_in, (0, units // 2), (width, units // 2)),
        (w_out, (0, 0), (units // 2, width)),
        (w_out, (units // 2, 0), (units // 2, width)),
    ):
        weights.append(load(array, at, shape))
    parts = {}
    for plane in range(2):
        blocks = order[plane * length : (plane + 1) * length]
        own, other, seat, gate = select([held[b] for b in blocks], count, cap, n_dev)
        came = lax.ppermute(other, axes, rings.partner)
        result = expert(own, came, weights)
        theirs = lax.ppermute(result, axes, rings.partner)
        sums = spread(result, theirs, seat, gate, count)
        for block, value in zip(blocks, sums, strict=True):
            parts[block] = [value]

    def total(block):
        value = parts[block][0].astype(jnp.float32)
        for more in parts[block][1:]:
            value = value + more.astype(jnp.float32)
        return value.astype(jnp.bfloat16)

    for channel, block in return_sequence():
        value = lax.ppermute(total(block), axes, inverse[channel])
        parts[seen_from_source(channel, block, length)].append(value)
    return total((0, 0))


def earlier_count(onehot):
    return jnp.cumsum(onehot, axis=0) - onehot


def contract_rows(left, right):
    return lax.dot_general(
        left,
        right,
        (((0,), (0,)), ((), ())),
        precision=lax.Precision.HIGHEST,
        preferred_element_type=jnp.float32,
    )


def expert_rows(slot_block, w_first, w_second):

    def one_block(rows_block):
        hidden = jnp.maximum(
            jnp.dot(rows_block, w_first, preferred_element_type=jnp.float32), 0.0
        ).astype(jnp.bfloat16)
        return jnp.dot(hidden, w_second, preferred_element_type=jnp.float32).astype(jnp.bfloat16)

    return lax.map(one_block, slot_block)


def seat_sources(seat_of, valid, seat_total):
    item_count = seat_of.shape[0]
    target_seat = jnp.where(valid, seat_of, seat_total)
    empty_seats = jnp.full((seat_total,), item_count, jnp.int32)
    return empty_seats.at[target_seat].set(jnp.arange(item_count, dtype=jnp.int32), mode="drop")


def per_device(tokens, expert_ids, gates, w_in, w_out):
    n_grp = lax.axis_size("grp")
    n_dev = lax.axis_size("dev")
    token_count, feature_width = tokens.shape
    cap_grp = min(token_count, 3 * ((4 * token_count + n_grp - 1) // n_grp))
    cap_exp = min(4 * token_count, 24 * token_count // n_dev)
    seat_total = n_dev * cap_exp
    zero_half = jnp.zeros((), jnp.bfloat16)
    w_first = w_in[0]
    w_second = w_out[0]
    pair_ids = expert_ids.reshape(token_count * 4, 2)
    pair_group = pair_ids[:, 0] // n_dev
    group_hot = (pair_group[:, None] == jnp.arange(n_grp)[None, :]).astype(jnp.int32)
    group_rank = jnp.sum(earlier_count(group_hot) * group_hot, axis=1)
    target = pair_group * cap_grp + group_rank
    slot_count = n_grp * cap_grp
    placed = (target[None, :] == jnp.arange(slot_count)[:, None]).astype(jnp.int32)
    token_hot = placed.reshape(slot_count, token_count, 4).sum(axis=2)
    rows_out = jnp.dot(
        token_hot.astype(jnp.bfloat16), tokens, preferred_element_type=jnp.float32
    ).astype(jnp.bfloat16)
    local_ids = pair_ids % n_dev
    picks_out = jnp.dot(placed, local_ids + 1) - 1
    gains_out = jnp.dot(
        placed.astype(jnp.bfloat16),
        gates.reshape(token_count * 4, 2),
        preferred_element_type=jnp.float32,
    ).astype(jnp.bfloat16)
    rows_in, picks_in, gains_in = (
        lax.all_to_all(
            rows_out.reshape(n_grp, cap_grp, feature_width),
            "grp",
            split_axis=0,
            concat_axis=0,
            tiled=True,
        ),
        lax.all_to_all(
            picks_out.reshape(n_grp, cap_grp, 2), "grp", split_axis=0, concat_axis=0, tiled=True
        ),
        lax.all_to_all(
            gains_out.reshape(n_grp, cap_grp, 2), "grp", split_axis=0, concat_axis=0, tiled=True
        ),
    )
    relay_rows = rows_in.reshape(slot_count, feature_width)
    relay_picks = picks_in.reshape(slot_count, 2)
    relay_gains = gains_in.reshape(slot_count, 2)
    live_count = 4 * token_count
    slot_live = (relay_picks[:, 0] >= 0).astype(jnp.int32)
    slot_order = jnp.cumsum(slot_live) - 1
    packed = (
        (slot_order[None, :] == jnp.arange(live_count)[:, None]) & (slot_live[None, :] > 0)
    ).astype(jnp.int32)
    packed_rows = jnp.dot(
        packed.astype(jnp.bfloat16), relay_rows, preferred_element_type=jnp.float32
    ).astype(jnp.bfloat16)
    packed_picks = jnp.dot(packed, relay_picks)
    packed_gains = jnp.dot(
        packed.astype(jnp.bfloat16), relay_gains, preferred_element_type=jnp.float32
    ).astype(jnp.bfloat16)
    group_rows, group_picks, group_gains = (
        lax.all_gather(packed_rows, "dev", axis=0, tiled=True),
        lax.all_gather(packed_picks, "dev", axis=0, tiled=True),
        lax.all_gather(packed_gains, "dev", axis=0, tiled=True),
    )
    gathered_count = group_rows.shape[0]
    chosen = jnp.sum((group_picks == lax.axis_index("dev")).astype(jnp.int32), axis=1)
    expert_seat = jnp.cumsum(chosen) - 1
    seat_source = seat_sources(expert_seat, chosen > 0, seat_total)
    seat_live = seat_source < gathered_count
    taken_rows = jnp.take(group_rows, jnp.minimum(seat_source, gathered_count - 1), axis=0)
    expert_in = jnp.where(seat_live[:, None], taken_rows, zero_half)
    expert_out = expert_rows(
        expert_in.reshape(n_dev, cap_exp, feature_width), w_first, w_second
    ).reshape(seat_total, feature_width)
    spread_rows = jnp.take(expert_out, jnp.clip(expert_seat, 0, seat_total - 1), axis=0)
    spread = jnp.where((chosen > 0)[:, None], spread_rows, zero_half)
    back = lax.all_to_all(
        spread.reshape(n_dev, live_count, feature_width),
        "dev",
        split_axis=0,
        concat_axis=0,
        tiled=True,
    )
    match = (packed_picks[None, :, :] == jnp.arange(n_dev)[:, None, None]).astype(jnp.float32)
    row_weights = jnp.sum(match * packed_gains.astype(jnp.float32)[None, :, :], axis=2)
    packed_sum = jnp.sum(row_weights[:, :, None] * back.astype(jnp.float32), axis=0)
    partial_value = contract_rows(packed.astype(jnp.float32), packed_sum)
    returned_sums = lax.all_to_all(
        partial_value.reshape(n_grp, cap_grp, feature_width),
        "grp",
        split_axis=0,
        concat_axis=0,
        tiled=True,
    )
    mixed = contract_rows(
        token_hot.astype(jnp.float32), returned_sums.reshape(slot_count, feature_width)
    )
    return mixed.astype(jnp.bfloat16)


def solution(mesh):
    rings = find_rings(mesh)
    if rings is None:
        return mapped(mesh, per_device)

    def body(*args):
        return on_rings(rings, *args)

    return mapped(mesh, body)


def mapped(mesh, body):
    return jax.shard_map(
        body,
        mesh=mesh,
        in_specs=(
            P(("grp", "dev"), None),
            P(("grp", "dev"), None),
            P(("grp", "dev"), None),
            P(("grp", "dev"), None, None),
            P(("grp", "dev"), None, None),
        ),
        out_specs=P(("grp", "dev"), None),
        check_vma=False,
    )
```

```python
import functools

import jax
import jax.numpy as jnp
from jax import lax
from jax.experimental import pallas as pl
from jax.experimental.pallas import tpu as pltpu
from jax.sharding import PartitionSpec as P


LANES = 128
SUB = 8
MIB = 1 << 20


class Rings:
    def __init__(self, length, clockwise, counter, mirror, partner):
        self.length = length
        self.perms = (clockwise, counter, mirror)
        self.partner = partner


def wrap(step, length):
    step %= length
    return step - length if step > length // 2 else step


def seen_from_source(channel, block, length):
    step, plane = block
    if channel == 0:
        return (wrap(step + 1, length), plane)
    if channel == 1:
        return (wrap(step - 1, length), plane)
    return (step, 1 - plane)


def gather_sequence():
    return (
        (0, (-1, 0)),
        (1, (1, 0)),
        (2, (0, 1)),
        (0, (-2, 0)),
        (1, (2, 0)),
        (2, (1, 1)),
        (0, (-3, 0)),
        (1, (3, 0)),
        (2, (-2, 1)),
        (0, (4, 0)),
        (1, (2, 1)),
        (0, (-3, 1)),
        (2, (-1, 1)),
        (2, (4, 1)),
        (2, (3, 1)),
    )


def return_sequence():
    return (
        (2, (4, 1)),
        (0, (-3, 1)),
        (1, (3, 1)),
        (2, (0, 1)),
        (0, (4, 0)),
        (2, (-2, 1)),
        (1, (2, 1)),
        (0, (-3, 0)),
        (1, (3, 0)),
        (2, (-1, 1)),
        (0, (-2, 0)),
        (1, (2, 0)),
        (2, (1, 1)),
        (0, (-1, 0)),
        (1, (1, 0)),
    )


def find_rings(mesh):
    grid = mesh.devices
    n_grp, n_dev = grid.shape
    if n_dev != 2 or not hasattr(grid[0, 0], "coords"):
        return None
    place = {}
    for g in range(n_grp):
        for d in range(n_dev):
            device = grid[g, d]
            place[(tuple(device.coords), device.core_on_chip)] = (g, d)
    planes = []
    for d in range(n_dev):
        planes.append(sorted({tuple(grid[g, d].coords) for g in range(n_grp)}))
    if 2 * len(planes[0]) != n_grp or set(planes[0]) & set(planes[1]):
        return None
    wide = [a for a in range(3) if len({c[a] for c in planes[0]}) == 2]
    flat = [a for a in range(3) if len({c[a] for c in planes[0]}) == 1]
    if not wide or len(flat) != 1:
        return None
    side = wide[0]
    along = [a for a in range(3) if a not in (side, flat[0])][0]
    low = min(c[side] for c in planes[0])
    up = sorted((c for c in planes[0] if c[side] == low), key=lambda c: c[along])
    down = sorted((c for c in planes[0] if c[side] != low), key=lambda c: -c[along])
    order = up + down
    length = len(order)
    if length != 8:
        return None

    def index(chip, core):
        g, d = place[(chip, core)]
        return g * n_dev + d

    def mirrored(chip):
        other = planes[1][0][flat[0]]
        return tuple(other if a == flat[0] else v for a, v in enumerate(chip))

    if any((mirrored(c), k) not in place or (c, k) not in place for c in order for k in range(2)):
        return None
    if any(place[(c, k)][0] != place[(mirrored(c), k)][0] for c in order for k in range(2)):
        return None
    clockwise, counter, mirror, partner = [], [], [], []
    for here in range(length):
        after = (here + 1) % length
        for core in range(2):
            for turn in (lambda c: c, mirrored):
                a, b = index(turn(order[here]), core), index(turn(order[after]), core)
                clockwise.append((a, b))
                counter.append((b, a))
                partner.append((a, index(turn(order[here]), 1 - core)))
            a, b = index(order[here], core), index(mirrored(order[here]), core)
            mirror += [(a, b), (b, a)]
    if any(mate != one ^ n_dev for one, mate in partner):
        return None
    return Rings(length, clockwise, counter, mirror, partner)


def pack_kernel(ids_hbm, gates_hbm, tokens_hbm, out_ref, ids_ref, gates_ref, sem, *, experts):
    count, width = tokens_hbm.shape
    picks = ids_ref.shape[0]
    copies = [
        pltpu.make_async_copy(tokens_hbm, out_ref.at[pl.ds(0, count)], sem.at[0]),
        pltpu.make_async_copy(ids_hbm, ids_ref, sem.at[1]),
        pltpu.make_async_copy(gates_hbm, gates_ref, sem.at[2]),
    ]
    for copy in copies:
        copy.start()
    row = lax.broadcasted_iota(jnp.int32, (experts, count), 0)
    table = jnp.zeros((experts, count), jnp.float32)
    copies[1].wait()
    copies[2].wait()
    ids = ids_ref[...]
    gates = gates_ref[...].astype(jnp.float32)
    for k in range(picks):
        table += jnp.where(ids[k : k + 1, :] == row, gates[k : k + 1, :], 0.0)
    twice = jnp.concatenate([table, table], axis=1).astype(jnp.bfloat16)
    out_ref[count:, :] = jnp.zeros((SUB, width), jnp.bfloat16)
    for q in range(experts // SUB):
        out_ref[count:, q * LANES : (q + 1) * LANES] = twice[q * SUB : (q + 1) * SUB, :]
    copies[0].wait()


def pack(ids, gates, tokens, experts):
    count, width = tokens.shape
    picks = ids.shape[1]
    return pl.pallas_call(
        functools.partial(pack_kernel, experts=experts),
        in_specs=[pl.BlockSpec(memory_space=pltpu.HBM)] * 3,
        out_shape=jax.ShapeDtypeStruct((count + SUB, width), jnp.bfloat16),
        scratch_shapes=[
            pltpu.VMEM((picks, count), jnp.int32),
            pltpu.VMEM((picks, count), jnp.bfloat16),
            pltpu.SemaphoreType.DMA((3,)),
        ],
        name="pack",
        compiler_params=pltpu.CompilerParams(vmem_limit_bytes=2 * MIB),
    )(*(pltpu.with_memory_space_constraint(x, pltpu.HBM) for x in (ids.T, gates.T, tokens)))


def one_hot(seat, cap):
    seats = lax.broadcasted_iota(jnp.int32, (cap, LANES), 0)
    return jnp.where(seats == seat, 1.0, 0.0)


def select_kernel(*refs, blocks, count, cap, stride):
    here = lax.axis_index("grp") * stride + lax.axis_index("dev")
    mate = here ^ stride
    block_refs = refs[:blocks]
    own_ref, other_ref, seat_ref, gate_ref = refs[-4:]
    pairs = blocks // 2
    dot = functools.partial(jnp.dot, preferred_element_type=jnp.float32)
    tails = jnp.concatenate([r[count:, :] for r in block_refs], axis=0)
    upper = (
        lax.broadcasted_iota(jnp.int32, (LANES, LANES), 0)
        < lax.broadcasted_iota(jnp.int32, (LANES, LANES), 1)
    ).astype(jnp.bfloat16)
    left = lax.broadcasted_iota(jnp.int32, (2 * pairs, 2 * pairs), 0)
    right = lax.broadcasted_iota(jnp.int32, (2 * pairs, 2 * pairs), 1)
    before = ((right < left) & (right // pairs == left // pairs)).astype(jnp.bfloat16)
    lane = lax.broadcasted_iota(jnp.int32, (pairs, LANES), 1)
    row_of = lax.broadcasted_iota(jnp.int32, (pairs, blocks * SUB), 0)
    col_of = lax.broadcasted_iota(jnp.int32, (pairs, blocks * SUB), 1)
    groups = tails.shape[1] // LANES
    rows = jnp.concatenate([r[:count, :] for r in block_refs], axis=0)
    picks = []
    for expert in (here, mate):
        sub = expert % SUB
        group = expert // SUB
        table = tails[:, :LANES]
        for q in range(1, groups):
            table = jnp.where(group == q, tails[:, q * LANES : (q + 1) * LANES], table)
        pick_a = (col_of == (2 * row_of) * SUB + sub).astype(jnp.bfloat16)
        pick_b = (col_of == (2 * row_of + 1) * SUB + sub).astype(jnp.bfloat16)
        picks.append(jnp.where(lane < count, dot(pick_a, table), dot(pick_b, table)))
    gate = jnp.concatenate(picks, axis=0)
    chosen = gate > 0.0
    ones = jnp.where(chosen, 1.0, 0.0)
    total = jnp.broadcast_to(jnp.sum(ones, axis=1, keepdims=True), (2 * pairs, LANES))
    spot = dot(ones.astype(jnp.bfloat16), upper) + dot(before, total.astype(jnp.bfloat16))
    spot = spot.astype(jnp.int32)
    seat = jnp.where(here < mate, spot, cap - 1 - spot)
    seat = jnp.where(chosen, seat, -1)
    for k, out_ref in enumerate((own_ref, other_ref)):
        mine = seat[k * pairs : (k + 1) * pairs, :]
        seat_ref[k] = mine
        gate_ref[k] = gate[k * pairs : (k + 1) * pairs, :]
        hot = jnp.concatenate([one_hot(mine[o : o + 1, :], cap) for o in range(pairs)], axis=1)
        out_ref[...] = dot(hot.astype(jnp.bfloat16), rows).astype(jnp.bfloat16)


def select(blocks, count, cap, stride):
    width = blocks[0].shape[1]
    pairs = len(blocks) // 2
    taken = jax.ShapeDtypeStruct((cap, width), jnp.bfloat16)
    vmem = pl.BlockSpec(memory_space=pltpu.VMEM)
    return pl.pallas_call(
        functools.partial(select_kernel, blocks=len(blocks), count=count, cap=cap, stride=stride),
        in_specs=[vmem] * len(blocks),
        out_shape=[
            taken,
            taken,
            jax.ShapeDtypeStruct((2, pairs, LANES), jnp.int32),
            jax.ShapeDtypeStruct((2, pairs, LANES), jnp.float32),
        ],
        name="select",
        compiler_params=pltpu.CompilerParams(vmem_limit_bytes=16 * MIB),
    )(*blocks)


def load_kernel(source, out_ref, sems, *, at):
    pieces = sems.shape[0]
    rows = out_ref.shape[0] // pieces
    copies = [
        pltpu.make_async_copy(
            source.at[0, pl.ds(at[0] + p * rows, rows), pl.ds(at[1], out_ref.shape[1])],
            out_ref.at[pl.ds(p * rows, rows)],
            sems.at[p],
        )
        for p in range(pieces)
    ]
    for copy in copies:
        copy.start()
    for copy in copies:
        copy.wait()


def load(weights, at, shape):
    return pl.pallas_call(
        functools.partial(load_kernel, at=at),
        in_specs=[pl.BlockSpec(memory_space=pltpu.HBM)],
        out_shape=jax.ShapeDtypeStruct(shape, weights.dtype),
        scratch_shapes=[pltpu.SemaphoreType.DMA((8,))],
        name="load",
        compiler_params=pltpu.CompilerParams(vmem_limit_bytes=4 * MIB),
    )(pltpu.with_memory_space_constraint(weights, pltpu.HBM))


def expert_kernel(own_ref, came_ref, in_a, out_a, out_ref):
    dot = functools.partial(jnp.dot, preferred_element_type=jnp.float32)
    rows = own_ref[...] + came_ref[...]
    result = None
    for first, second in ((in_a, out_a),):
        hidden = jnp.maximum(dot(rows, first[...]), 0.0).astype(jnp.bfloat16)
        part = dot(hidden, second[...])
        result = part if result is None else result + part
    out_ref[...] = result.astype(jnp.bfloat16)


def expert(own, came, weights):
    vmem = pl.BlockSpec(memory_space=pltpu.VMEM)
    return pl.pallas_call(
        expert_kernel,
        in_specs=[vmem] * (2 + len(weights)),
        out_shape=jax.ShapeDtypeStruct(own.shape, jnp.bfloat16),
        name="expert",
        compiler_params=pltpu.CompilerParams(vmem_limit_bytes=16 * MIB),
    )(own, came, *weights)


def spread_kernel(own_ref, came_ref, seat_ref, gate_ref, *out_refs, count, cap):
    pairs = seat_ref.shape[1]
    value = None
    for k, ref in enumerate((own_ref, came_ref)):
        weights = jnp.concatenate(
            [
                one_hot(seat_ref[k, o : o + 1, :], cap) * gate_ref[k, o : o + 1, :]
                for o in range(pairs)
            ],
            axis=1,
        ).astype(jnp.bfloat16)
        part = lax.dot_general(
            weights, ref[...], (((0,), (0,)), ((), ())), preferred_element_type=jnp.float32
        )
        value = part if value is None else value + part
    value = value.astype(jnp.bfloat16)
    for o, out_ref in enumerate(out_refs):
        out_ref[...] = value[o * count : (o + 1) * count, :]


def spread(own, came, seat, gate, count):
    blocks = 2 * seat.shape[1]
    cap, width = own.shape
    out = jax.ShapeDtypeStruct((count, width), jnp.bfloat16)
    return pl.pallas_call(
        functools.partial(spread_kernel, count=count, cap=cap),
        out_shape=[out] * blocks,
        name="spread",
        compiler_params=pltpu.CompilerParams(vmem_limit_bytes=12 * MIB),
    )(own, came, seat, gate)


def on_rings(rings, tokens, expert_ids, gates, w_in, w_out):
    axes = ("grp", "dev")
    n_dev = lax.axis_size("dev")
    experts = lax.axis_size("grp") * n_dev
    count, width = tokens.shape
    length = rings.length
    if 2 * count != LANES or length % 4 or experts % SUB or experts * LANES > SUB * width:
        return per_device(tokens, expert_ids, gates, w_in, w_out)
    inverse = (rings.perms[1], rings.perms[0], rings.perms[2])
    held = {(0, 0): pack(expert_ids, gates, tokens, experts)}
    for channel, block in gather_sequence():
        source = held[seen_from_source(channel, block, length)]
        held[block] = lax.ppermute(source, axes, rings.perms[channel])
    order = sorted(held, key=lambda b: (b[1], b[0]))
    cap = 4 * count
    units = w_in.shape[2]
    weights = []
    for array, at, shape in (
        (w_in, (0, 0), (width, units)),
        (w_out, (0, 0), (units, width)),
    ):
        weights.append(load(array, at, shape))
    parts = {}
    for plane in range(2):
        blocks = order[plane * length : (plane + 1) * length]
        own, other, seat, gate = select([held[b] for b in blocks], count, cap, n_dev)
        came = lax.ppermute(other, axes, rings.partner)
        result = expert(own, came, weights)
        theirs = lax.ppermute(result, axes, rings.partner)
        sums = spread(result, theirs, seat, gate, count)
        for block, value in zip(blocks, sums, strict=True):
            parts[block] = [value]

    def total(block):
        value = parts[block][0].astype(jnp.float32)
        for more in parts[block][1:]:
            value = value + more.astype(jnp.float32)
        return value.astype(jnp.bfloat16)

    for channel, block in return_sequence():
        value = lax.ppermute(total(block), axes, inverse[channel])
        parts[seen_from_source(channel, block, length)].append(value)
    return total((0, 0))


def earlier_count(onehot):
    return jnp.cumsum(onehot, axis=0) - onehot


def contract_rows(left, right):
    return lax.dot_general(
        left,
        right,
        (((0,), (0,)), ((), ())),
        precision=lax.Precision.HIGHEST,
        preferred_element_type=jnp.float32,
    )


def expert_rows(slot_block, w_first, w_second):

    def one_block(rows_block):
        hidden = jnp.maximum(
            jnp.dot(rows_block, w_first, preferred_element_type=jnp.float32), 0.0
        ).astype(jnp.bfloat16)
        return jnp.dot(hidden, w_second, preferred_element_type=jnp.float32).astype(jnp.bfloat16)

    return lax.map(one_block, slot_block)


def seat_sources(seat_of, valid, seat_total):
    item_count = seat_of.shape[0]
    target_seat = jnp.where(valid, seat_of, seat_total)
    empty_seats = jnp.full((seat_total,), item_count, jnp.int32)
    return empty_seats.at[target_seat].set(jnp.arange(item_count, dtype=jnp.int32), mode="drop")


def per_device(tokens, expert_ids, gates, w_in, w_out):
    n_grp = lax.axis_size("grp")
    n_dev = lax.axis_size("dev")
    token_count, feature_width = tokens.shape
    cap_grp = min(token_count, 3 * ((4 * token_count + n_grp - 1) // n_grp))
    cap_exp = min(4 * token_count, 24 * token_count // n_dev)
    seat_total = n_dev * cap_exp
    zero_half = jnp.zeros((), jnp.bfloat16)
    w_first = w_in[0]
    w_second = w_out[0]
    pair_ids = expert_ids.reshape(token_count * 4, 2)
    pair_group = pair_ids[:, 0] // n_dev
    group_hot = (pair_group[:, None] == jnp.arange(n_grp)[None, :]).astype(jnp.int32)
    group_rank = jnp.sum(earlier_count(group_hot) * group_hot, axis=1)
    target = pair_group * cap_grp + group_rank
    slot_count = n_grp * cap_grp
    placed = (target[None, :] == jnp.arange(slot_count)[:, None]).astype(jnp.int32)
    token_hot = placed.reshape(slot_count, token_count, 4).sum(axis=2)
    rows_out = jnp.dot(
        token_hot.astype(jnp.bfloat16), tokens, preferred_element_type=jnp.float32
    ).astype(jnp.bfloat16)
    local_ids = pair_ids % n_dev
    picks_out = jnp.dot(placed, local_ids + 1) - 1
    gains_out = jnp.dot(
        placed.astype(jnp.bfloat16),
        gates.reshape(token_count * 4, 2),
        preferred_element_type=jnp.float32,
    ).astype(jnp.bfloat16)
    rows_in, picks_in, gains_in = (
        lax.all_to_all(
            rows_out.reshape(n_grp, cap_grp, feature_width),
            "grp",
            split_axis=0,
            concat_axis=0,
            tiled=True,
        ),
        lax.all_to_all(
            picks_out.reshape(n_grp, cap_grp, 2), "grp", split_axis=0, concat_axis=0, tiled=True
        ),
        lax.all_to_all(
            gains_out.reshape(n_grp, cap_grp, 2), "grp", split_axis=0, concat_axis=0, tiled=True
        ),
    )
    relay_rows = rows_in.reshape(slot_count, feature_width)
    relay_picks = picks_in.reshape(slot_count, 2)
    relay_gains = gains_in.reshape(slot_count, 2)
    live_count = 4 * token_count
    slot_live = (relay_picks[:, 0] >= 0).astype(jnp.int32)
    slot_order = jnp.cumsum(slot_live) - 1
    packed = (
        (slot_order[None, :] == jnp.arange(live_count)[:, None]) & (slot_live[None, :] > 0)
    ).astype(jnp.int32)
    packed_rows = jnp.dot(
        packed.astype(jnp.bfloat16), relay_rows, preferred_element_type=jnp.float32
    ).astype(jnp.bfloat16)
    packed_picks = jnp.dot(packed, relay_picks)
    packed_gains = jnp.dot(
        packed.astype(jnp.bfloat16), relay_gains, preferred_element_type=jnp.float32
    ).astype(jnp.bfloat16)
    group_rows, group_picks, group_gains = (
        lax.all_gather(packed_rows, "dev", axis=0, tiled=True),
        lax.all_gather(packed_picks, "dev", axis=0, tiled=True),
        lax.all_gather(packed_gains, "dev", axis=0, tiled=True),
    )
    gathered_count = group_rows.shape[0]
    chosen = jnp.sum((group_picks == lax.axis_index("dev")).astype(jnp.int32), axis=1)
    expert_seat = jnp.cumsum(chosen) - 1
    seat_source = seat_sources(expert_seat, chosen > 0, seat_total)
    seat_live = seat_source < gathered_count
    taken_rows = jnp.take(group_rows, jnp.minimum(seat_source, gathered_count - 1), axis=0)
    expert_in = jnp.where(seat_live[:, None], taken_rows, zero_half)
    expert_out = expert_rows(
        expert_in.reshape(n_dev, cap_exp, feature_width), w_first, w_second
    ).reshape(seat_total, feature_width)
    spread_rows = jnp.take(expert_out, jnp.clip(expert_seat, 0, seat_total - 1), axis=0)
    spread = jnp.where((chosen > 0)[:, None], spread_rows, zero_half)
    back = lax.all_to_all(
        spread.reshape(n_dev, live_count, feature_width),
        "dev",
        split_axis=0,
        concat_axis=0,
        tiled=True,
    )
    match = (packed_picks[None, :, :] == jnp.arange(n_dev)[:, None, None]).astype(jnp.float32)
    row_weights = jnp.sum(match * packed_gains.astype(jnp.float32)[None, :, :], axis=2)
    packed_sum = jnp.sum(row_weights[:, :, None] * back.astype(jnp.float32), axis=0)
    partial_value = contract_rows(packed.astype(jnp.float32), packed_sum)
    returned_sums = lax.all_to_all(
        partial_value.reshape(n_grp, cap_grp, feature_width),
        "grp",
        split_axis=0,
        concat_axis=0,
        tiled=True,
    )
    mixed = contract_rows(
        token_hot.astype(jnp.float32), returned_sums.reshape(slot_count, feature_width)
    )
    return mixed.astype(jnp.bfloat16)


def solution(mesh):
    rings = find_rings(mesh)
    if rings is None:
        return mapped(mesh, per_device)

    def body(*args):
        return on_rings(rings, *args)

    return mapped(mesh, body)


def mapped(mesh, body):
    return jax.shard_map(
        body,
        mesh=mesh,
        in_specs=(
            P(("grp", "dev"), None),
            P(("grp", "dev"), None),
            P(("grp", "dev"), None),
            P(("grp", "dev"), None, None),
            P(("grp", "dev"), None, None),
        ),
        out_specs=P(("grp", "dev"), None),
        check_vma=False,
    )
```

```python
import functools

import jax
import jax.numpy as jnp
from jax import lax
from jax.experimental import pallas as pl
from jax.experimental.pallas import tpu as pltpu
from jax.sharding import PartitionSpec as P


LANES = 128
SUB = 8
MIB = 1 << 20


class Rings:
    def __init__(self, ring, mirror, partner):
        self.ring = ring
        self.back = [(b, a) for a, b in ring]
        self.mirror = mirror
        self.partner = partner


def find_rings(mesh):
    grid = mesh.devices
    n_grp, n_dev = grid.shape
    if n_dev != 2 or not hasattr(grid[0, 0], "coords"):
        return None
    place = {}
    for g in range(n_grp):
        for d in range(n_dev):
            device = grid[g, d]
            place[(tuple(device.coords), device.core_on_chip)] = (g, d)
    planes = []
    for d in range(n_dev):
        planes.append(sorted({tuple(grid[g, d].coords) for g in range(n_grp)}))
    if 2 * len(planes[0]) != n_grp or set(planes[0]) & set(planes[1]):
        return None
    wide = [a for a in range(3) if len({c[a] for c in planes[0]}) == 2]
    flat = [a for a in range(3) if len({c[a] for c in planes[0]}) == 1]
    if not wide or len(flat) != 1:
        return None
    side = wide[0]
    along = [a for a in range(3) if a not in (side, flat[0])][0]
    low = min(c[side] for c in planes[0])
    up = sorted((c for c in planes[0] if c[side] == low), key=lambda c: c[along])
    down = sorted((c for c in planes[0] if c[side] != low), key=lambda c: -c[along])
    order = up + down
    length = len(order)
    if length != 8:
        return None

    def index(chip, core):
        g, d = place[(chip, core)]
        return g * n_dev + d

    def mirrored(chip):
        other = planes[1][0][flat[0]]
        return tuple(other if a == flat[0] else v for a, v in enumerate(chip))

    if any((mirrored(c), k) not in place or (c, k) not in place for c in order for k in range(2)):
        return None
    if any(place[(c, k)][0] != place[(mirrored(c), k)][0] for c in order for k in range(2)):
        return None
    ring, mirror, partner = [], [], []
    for here in range(length):
        after = (here + 1) % length
        for core in range(2):
            for turn in (lambda c: c, mirrored):
                a, b = index(turn(order[here]), core), index(turn(order[after]), core)
                ring.append((b, a) if core else (a, b))
                partner.append((a, index(turn(order[here]), 1 - core)))
            a, b = index(order[here], core), index(mirrored(order[here]), core)
            mirror += [(a, b), (b, a)]
    if any(mate != one ^ n_dev for one, mate in partner):
        return None
    return Rings(ring, mirror, partner)


def pack_kernel(ids_hbm, gates_hbm, tokens_hbm, out_ref, ids_ref, gates_ref, sem, *, experts):
    count, width = tokens_hbm.shape
    picks = ids_ref.shape[0]
    copies = [
        pltpu.make_async_copy(tokens_hbm, out_ref.at[pl.ds(0, count)], sem.at[0]),
        pltpu.make_async_copy(ids_hbm, ids_ref, sem.at[1]),
        pltpu.make_async_copy(gates_hbm, gates_ref, sem.at[2]),
    ]
    for copy in copies:
        copy.start()
    row = lax.broadcasted_iota(jnp.int32, (experts, count), 0)
    table = jnp.zeros((experts, count), jnp.float32)
    copies[1].wait()
    copies[2].wait()
    ids = ids_ref[...]
    gates = gates_ref[...].astype(jnp.float32)
    for k in range(picks):
        table += jnp.where(ids[k : k + 1, :] == row, gates[k : k + 1, :], 0.0)
    twice = jnp.concatenate([table, table], axis=1).astype(jnp.bfloat16)
    out_ref[count:, :] = jnp.zeros((SUB, width), jnp.bfloat16)
    for q in range(experts // SUB):
        out_ref[count:, q * LANES : (q + 1) * LANES] = twice[q * SUB : (q + 1) * SUB, :]
    copies[0].wait()


def pack(ids, gates, tokens, experts):
    count, width = tokens.shape
    picks = ids.shape[1]
    return pl.pallas_call(
        functools.partial(pack_kernel, experts=experts),
        in_specs=[pl.BlockSpec(memory_space=pltpu.HBM)] * 3,
        out_shape=jax.ShapeDtypeStruct((count + SUB, width), jnp.bfloat16),
        scratch_shapes=[
            pltpu.VMEM((picks, count), jnp.int32),
            pltpu.VMEM((picks, count), jnp.bfloat16),
            pltpu.SemaphoreType.DMA((3,)),
        ],
        name="pack",
        compiler_params=pltpu.CompilerParams(vmem_limit_bytes=2 * MIB),
    )(*(pltpu.with_memory_space_constraint(x, pltpu.HBM) for x in (ids.T, gates.T, tokens)))


def one_hot(seat, cap):
    seats = lax.broadcasted_iota(jnp.int32, (cap, LANES), 0)
    return jnp.where(seats == seat, 1.0, 0.0)


def select_kernel(*refs, count, cap, stride):
    here = lax.axis_index("grp") * stride + lax.axis_index("dev")
    mate = here ^ stride
    own_ref, other_ref, seat_ref, gate_ref = refs[-4:]
    each = count + SUB
    pieces = [(r, at) for r in refs[:-4] for at in range(0, r.shape[0], each)]
    blocks = len(pieces)
    pairs = blocks // 2
    dot = functools.partial(jnp.dot, preferred_element_type=jnp.float32)
    tails = jnp.concatenate([r[at + count : at + each, :] for r, at in pieces], axis=0)
    upper = (
        lax.broadcasted_iota(jnp.int32, (LANES, LANES), 0)
        < lax.broadcasted_iota(jnp.int32, (LANES, LANES), 1)
    ).astype(jnp.bfloat16)
    left = lax.broadcasted_iota(jnp.int32, (2 * pairs, 2 * pairs), 0)
    right = lax.broadcasted_iota(jnp.int32, (2 * pairs, 2 * pairs), 1)
    before = ((right < left) & (right // pairs == left // pairs)).astype(jnp.bfloat16)
    lane = lax.broadcasted_iota(jnp.int32, (pairs, LANES), 1)
    row_of = lax.broadcasted_iota(jnp.int32, (pairs, blocks * SUB), 0)
    col_of = lax.broadcasted_iota(jnp.int32, (pairs, blocks * SUB), 1)
    groups = tails.shape[1] // LANES
    rows = jnp.concatenate([r[at : at + count, :] for r, at in pieces], axis=0)
    picks = []
    for expert in (here, mate):
        sub = expert % SUB
        group = expert // SUB
        table = tails[:, :LANES]
        for q in range(1, groups):
            table = jnp.where(group == q, tails[:, q * LANES : (q + 1) * LANES], table)
        pick_a = (col_of == (2 * row_of) * SUB + sub).astype(jnp.bfloat16)
        pick_b = (col_of == (2 * row_of + 1) * SUB + sub).astype(jnp.bfloat16)
        picks.append(jnp.where(lane < count, dot(pick_a, table), dot(pick_b, table)))
    gate = jnp.concatenate(picks, axis=0)
    chosen = gate > 0.0
    ones = jnp.where(chosen, 1.0, 0.0)
    total = jnp.broadcast_to(jnp.sum(ones, axis=1, keepdims=True), (2 * pairs, LANES))
    spot = dot(ones.astype(jnp.bfloat16), upper) + dot(before, total.astype(jnp.bfloat16))
    spot = spot.astype(jnp.int32)
    seat = jnp.where(here < mate, spot, cap - 1 - spot)
    seat = jnp.where(chosen, seat, -1)
    for k, out_ref in enumerate((own_ref, other_ref)):
        mine = seat[k * pairs : (k + 1) * pairs, :]
        seat_ref[k] = mine
        gate_ref[k] = gate[k * pairs : (k + 1) * pairs, :]
        hot = jnp.concatenate([one_hot(mine[o : o + 1, :], cap) for o in range(pairs)], axis=1)
        out_ref[...] = dot(hot.astype(jnp.bfloat16), rows).astype(jnp.bfloat16)


def select(blocks, count, cap, stride):
    width = blocks[0].shape[1]
    pairs = sum(b.shape[0] for b in blocks) // (2 * (count + SUB))
    taken = jax.ShapeDtypeStruct((cap, width), jnp.bfloat16)
    return pl.pallas_call(
        functools.partial(select_kernel, count=count, cap=cap, stride=stride),
        in_specs=[pl.BlockSpec(memory_space=pltpu.VMEM)] * len(blocks),
        out_shape=[
            taken,
            taken,
            jax.ShapeDtypeStruct((2, pairs, LANES), jnp.int32),
            jax.ShapeDtypeStruct((2, pairs, LANES), jnp.float32),
        ],
        name="select",
        compiler_params=pltpu.CompilerParams(vmem_limit_bytes=16 * MIB),
    )(*blocks)


def load_kernel(source, out_ref, sems, *, at):
    pieces = sems.shape[0]
    rows = out_ref.shape[0] // pieces
    copies = [
        pltpu.make_async_copy(
            source.at[0, pl.ds(at[0] + p * rows, rows), pl.ds(at[1], out_ref.shape[1])],
            out_ref.at[pl.ds(p * rows, rows)],
            sems.at[p],
        )
        for p in range(pieces)
    ]
    for copy in copies:
        copy.start()
    for copy in copies:
        copy.wait()


def load(weights, at, shape):
    return pl.pallas_call(
        functools.partial(load_kernel, at=at),
        in_specs=[pl.BlockSpec(memory_space=pltpu.HBM)],
        out_shape=jax.ShapeDtypeStruct(shape, weights.dtype),
        scratch_shapes=[pltpu.SemaphoreType.DMA((8,))],
        name="load",
        compiler_params=pltpu.CompilerParams(vmem_limit_bytes=4 * MIB),
    )(pltpu.with_memory_space_constraint(weights, pltpu.HBM))


def expert_kernel(own_ref, came_ref, first_ref, second_ref, out_ref):
    rows = own_ref[...] + came_ref[...]
    hidden = jnp.dot(rows, first_ref[...], preferred_element_type=jnp.float32)
    hidden = jnp.maximum(hidden, 0.0).astype(jnp.bfloat16)
    result = jnp.dot(hidden, second_ref[...], preferred_element_type=jnp.float32)
    out_ref[...] = result.astype(jnp.bfloat16)


def expert(own, came, first, second):
    vmem = pl.BlockSpec(memory_space=pltpu.VMEM)
    return pl.pallas_call(
        expert_kernel,
        in_specs=[vmem] * 4,
        out_shape=jax.ShapeDtypeStruct(own.shape, jnp.bfloat16),
        name="expert",
        compiler_params=pltpu.CompilerParams(vmem_limit_bytes=16 * MIB),
    )(own, came, first, second)


def spread_kernel(own_ref, came_ref, seat_ref, gate_ref, *out_refs, cap):
    pairs = seat_ref.shape[1]
    value = None
    for k, ref in enumerate((own_ref, came_ref)):
        weights = jnp.concatenate(
            [
                one_hot(seat_ref[k, o : o + 1, :], cap) * gate_ref[k, o : o + 1, :]
                for o in range(pairs)
            ],
            axis=1,
        ).astype(jnp.bfloat16)
        part = lax.dot_general(
            weights, ref[...], (((0,), (0,)), ((), ())), preferred_element_type=jnp.float32
        )
        value = part if value is None else value + part
    value = value.astype(jnp.bfloat16)
    at = 0
    for out_ref in out_refs:
        out_ref[...] = value[at : at + out_ref.shape[0], :]
        at += out_ref.shape[0]


def spread(own, came, seat, gate, sizes):
    cap, width = own.shape
    return pl.pallas_call(
        functools.partial(spread_kernel, cap=cap),
        out_shape=[jax.ShapeDtypeStruct((size, width), jnp.bfloat16) for size in sizes],
        name="spread",
        compiler_params=pltpu.CompilerParams(vmem_limit_bytes=12 * MIB),
    )(own, came, seat, gate)


def total(*values):
    result = values[0].astype(jnp.float32)
    for more in values[1:]:
        result = result + more.astype(jnp.float32)
    return result.astype(jnp.bfloat16)


def on_rings(rings, tokens, expert_ids, gates, w_in, w_out):
    axes = ("grp", "dev")
    n_dev = lax.axis_size("dev")
    experts = lax.axis_size("grp") * n_dev
    count, width = tokens.shape
    if 2 * count != LANES or experts % SUB or experts * LANES > SUB * width:
        return per_device(tokens, expert_ids, gates, w_in, w_out)

    def send(value, pairs):
        return lax.ppermute(value, axes, pairs)

    own = pack(expert_ids, gates, tokens, experts)
    half = own.shape[0]
    swapped = send(own, rings.partner)
    y0 = send(own, rings.mirror)
    r1 = send(jnp.concatenate([own, swapped], axis=0), rings.ring)
    y1 = send(r1, rings.mirror)
    r2 = send(r1, rings.ring)
    y2 = send(r2, rings.mirror)
    r3 = send(r2, rings.ring)
    r4 = send(r3[:half], rings.ring)
    y4 = send(r4, rings.mirror)
    y3 = send(y2, rings.ring)

    units = w_in.shape[2]
    first = load(w_in, (0, 0), (width, units))
    second = load(w_out, (0, 0), (units, width))
    cap = 4 * count
    sizes = (count, count, 2 * count, 2 * count, 2 * count)
    sums = []
    for blocks in ((own, r4, r1, r2, r3), (y0, y4, y1, y2, y3)):
        mine, other, seat, gate = select(blocks, count, cap, n_dev)
        came = send(other, rings.partner)
        result = expert(mine, came, first, second)
        theirs = send(result, rings.partner)
        sums.append(spread(result, theirs, seat, gate, sizes))
    (s0, s4, s1, s2, s3), (t0, t4, t1, t2, t3) = sums

    from_y3 = send(t3, rings.back)
    from_y4 = send(t4, rings.mirror)
    from_y2 = send(total(t2, from_y3), rings.mirror)
    from_r4 = send(total(s4, from_y4), rings.back)
    s3 = jnp.concatenate([total(s3[:count], from_r4), s3[count:]], axis=0)
    from_r3 = send(s3, rings.back)
    from_y1 = send(t1, rings.mirror)
    from_r2 = send(total(s2, from_r3, from_y2), rings.back)
    from_y0 = send(t0, rings.mirror)
    from_r1 = send(total(s1, from_r2, from_y1), rings.back)
    swapped = send(from_r1[count:], rings.partner)
    return total(s0, from_y0, from_r1[:count], swapped)


def earlier_count(onehot):
    return jnp.cumsum(onehot, axis=0) - onehot


def contract_rows(left, right):
    return lax.dot_general(
        left,
        right,
        (((0,), (0,)), ((), ())),
        precision=lax.Precision.HIGHEST,
        preferred_element_type=jnp.float32,
    )


def expert_rows(slot_block, w_first, w_second):

    def one_block(rows_block):
        hidden = jnp.maximum(
            jnp.dot(rows_block, w_first, preferred_element_type=jnp.float32), 0.0
        ).astype(jnp.bfloat16)
        return jnp.dot(hidden, w_second, preferred_element_type=jnp.float32).astype(jnp.bfloat16)

    return lax.map(one_block, slot_block)


def seat_sources(seat_of, valid, seat_total):
    item_count = seat_of.shape[0]
    target_seat = jnp.where(valid, seat_of, seat_total)
    empty_seats = jnp.full((seat_total,), item_count, jnp.int32)
    return empty_seats.at[target_seat].set(jnp.arange(item_count, dtype=jnp.int32), mode="drop")


def per_device(tokens, expert_ids, gates, w_in, w_out):
    n_grp = lax.axis_size("grp")
    n_dev = lax.axis_size("dev")
    token_count, feature_width = tokens.shape
    cap_grp = min(token_count, 3 * ((4 * token_count + n_grp - 1) // n_grp))
    cap_exp = min(4 * token_count, 24 * token_count // n_dev)
    seat_total = n_dev * cap_exp
    zero_half = jnp.zeros((), jnp.bfloat16)
    w_first = w_in[0]
    w_second = w_out[0]
    pair_ids = expert_ids.reshape(token_count * 4, 2)
    pair_group = pair_ids[:, 0] // n_dev
    group_hot = (pair_group[:, None] == jnp.arange(n_grp)[None, :]).astype(jnp.int32)
    group_rank = jnp.sum(earlier_count(group_hot) * group_hot, axis=1)
    target = pair_group * cap_grp + group_rank
    slot_count = n_grp * cap_grp
    placed = (target[None, :] == jnp.arange(slot_count)[:, None]).astype(jnp.int32)
    token_hot = placed.reshape(slot_count, token_count, 4).sum(axis=2)
    rows_out = jnp.dot(
        token_hot.astype(jnp.bfloat16), tokens, preferred_element_type=jnp.float32
    ).astype(jnp.bfloat16)
    local_ids = pair_ids % n_dev
    picks_out = jnp.dot(placed, local_ids + 1) - 1
    gains_out = jnp.dot(
        placed.astype(jnp.bfloat16),
        gates.reshape(token_count * 4, 2),
        preferred_element_type=jnp.float32,
    ).astype(jnp.bfloat16)
    rows_in, picks_in, gains_in = (
        lax.all_to_all(
            rows_out.reshape(n_grp, cap_grp, feature_width),
            "grp",
            split_axis=0,
            concat_axis=0,
            tiled=True,
        ),
        lax.all_to_all(
            picks_out.reshape(n_grp, cap_grp, 2), "grp", split_axis=0, concat_axis=0, tiled=True
        ),
        lax.all_to_all(
            gains_out.reshape(n_grp, cap_grp, 2), "grp", split_axis=0, concat_axis=0, tiled=True
        ),
    )
    relay_rows = rows_in.reshape(slot_count, feature_width)
    relay_picks = picks_in.reshape(slot_count, 2)
    relay_gains = gains_in.reshape(slot_count, 2)
    live_count = 4 * token_count
    slot_live = (relay_picks[:, 0] >= 0).astype(jnp.int32)
    slot_order = jnp.cumsum(slot_live) - 1
    packed = (
        (slot_order[None, :] == jnp.arange(live_count)[:, None]) & (slot_live[None, :] > 0)
    ).astype(jnp.int32)
    packed_rows = jnp.dot(
        packed.astype(jnp.bfloat16), relay_rows, preferred_element_type=jnp.float32
    ).astype(jnp.bfloat16)
    packed_picks = jnp.dot(packed, relay_picks)
    packed_gains = jnp.dot(
        packed.astype(jnp.bfloat16), relay_gains, preferred_element_type=jnp.float32
    ).astype(jnp.bfloat16)
    group_rows, group_picks, group_gains = (
        lax.all_gather(packed_rows, "dev", axis=0, tiled=True),
        lax.all_gather(packed_picks, "dev", axis=0, tiled=True),
        lax.all_gather(packed_gains, "dev", axis=0, tiled=True),
    )
    gathered_count = group_rows.shape[0]
    chosen = jnp.sum((group_picks == lax.axis_index("dev")).astype(jnp.int32), axis=1)
    expert_seat = jnp.cumsum(chosen) - 1
    seat_source = seat_sources(expert_seat, chosen > 0, seat_total)
    seat_live = seat_source < gathered_count
    taken_rows = jnp.take(group_rows, jnp.minimum(seat_source, gathered_count - 1), axis=0)
    expert_in = jnp.where(seat_live[:, None], taken_rows, zero_half)
    expert_out = expert_rows(
        expert_in.reshape(n_dev, cap_exp, feature_width), w_first, w_second
    ).reshape(seat_total, feature_width)
    spread_rows = jnp.take(expert_out, jnp.clip(expert_seat, 0, seat_total - 1), axis=0)
    spread = jnp.where((chosen > 0)[:, None], spread_rows, zero_half)
    back = lax.all_to_all(
        spread.reshape(n_dev, live_count, feature_width),
        "dev",
        split_axis=0,
        concat_axis=0,
        tiled=True,
    )
    match = (packed_picks[None, :, :] == jnp.arange(n_dev)[:, None, None]).astype(jnp.float32)
    row_weights = jnp.sum(match * packed_gains.astype(jnp.float32)[None, :, :], axis=2)
    packed_sum = jnp.sum(row_weights[:, :, None] * back.astype(jnp.float32), axis=0)
    partial_value = contract_rows(packed.astype(jnp.float32), packed_sum)
    returned_sums = lax.all_to_all(
        partial_value.reshape(n_grp, cap_grp, feature_width),
        "grp",
        split_axis=0,
        concat_axis=0,
        tiled=True,
    )
    mixed = contract_rows(
        token_hot.astype(jnp.float32), returned_sums.reshape(slot_count, feature_width)
    )
    return mixed.astype(jnp.bfloat16)


def solution(mesh):
    rings = find_rings(mesh)
    if rings is None:
        return mapped(mesh, per_device)

    def body(*args):
        return on_rings(rings, *args)

    return mapped(mesh, body)


def mapped(mesh, body):
    return jax.shard_map(
        body,
        mesh=mesh,
        in_specs=(
            P(("grp", "dev"), None),
            P(("grp", "dev"), None),
            P(("grp", "dev"), None),
            P(("grp", "dev"), None, None),
            P(("grp", "dev"), None, None),
        ),
        out_specs=P(("grp", "dev"), None),
        check_vma=False,
    )
```

```python
import functools

import jax
import jax.numpy as jnp
from jax import lax
from jax.experimental import pallas as pl
from jax.experimental.pallas import tpu as pltpu
from jax.sharding import PartitionSpec as P


LANES = 128
SUB = 8
MIB = 1 << 20
RETURN = (
    (2, ((4, 1),)),
    (0, ((-3, 1),)),
    (1, ((3, 1),)),
    (2, ((0, 1),)),
    (0, ((4, 0),)),
    (2, ((-2, 1),)),
    (1, ((2, 1),)),
    (0, ((-3, 0),)),
    (1, ((3, 0),)),
    (2, ((-1, 1),)),
    (0, ((-2, 0),)),
    (1, ((2, 0),)),
    (2, ((1, 1),)),
    (0, ((-1, 0),)),
    (1, ((1, 0),)),
)
GATHER = (
    (0, ((-1, 0),)),
    (1, ((1, 0),)),
    (2, ((0, 1),)),
    (0, ((-2, 0),)),
    (1, ((2, 0),)),
    (2, ((1, 1), (-1, 1))),
    (0, ((-3, 0),)),
    (1, ((3, 0),)),
    (2, ((2, 1),)),
    (0, ((4, 0),)),
    (2, ((3, 1), (-3, 1))),
    (0, ((-2, 1),)),
    (2, ((4, 1),)),
)


class Rings:
    def __init__(self, length, clockwise, counter, mirror, partner):
        self.length = length
        self.perms = (clockwise, counter, mirror)
        self.partner = partner


def wrap(step, length):
    step %= length
    return step - length if step > length // 2 else step


def seen_from_source(channel, block, length):
    step, plane = block
    if channel == 0:
        return (wrap(step + 1, length), plane)
    if channel == 1:
        return (wrap(step - 1, length), plane)
    return (step, 1 - plane)


def gather_sequence():
    return GATHER


def return_sequence():
    return RETURN


def find_rings(mesh):
    grid = mesh.devices
    n_grp, n_dev = grid.shape
    if n_dev != 2 or not hasattr(grid[0, 0], "coords"):
        return None
    place = {}
    for g in range(n_grp):
        for d in range(n_dev):
            device = grid[g, d]
            place[(tuple(device.coords), device.core_on_chip)] = (g, d)
    planes = []
    for d in range(n_dev):
        planes.append(sorted({tuple(grid[g, d].coords) for g in range(n_grp)}))
    if 2 * len(planes[0]) != n_grp or set(planes[0]) & set(planes[1]):
        return None
    wide = [a for a in range(3) if len({c[a] for c in planes[0]}) == 2]
    flat = [a for a in range(3) if len({c[a] for c in planes[0]}) == 1]
    if not wide or len(flat) != 1:
        return None
    side = wide[0]
    along = [a for a in range(3) if a not in (side, flat[0])][0]
    low = min(c[side] for c in planes[0])
    up = sorted((c for c in planes[0] if c[side] == low), key=lambda c: c[along])
    down = sorted((c for c in planes[0] if c[side] != low), key=lambda c: -c[along])
    order = up + down
    length = len(order)
    if length != 8:
        return None

    def index(chip, core):
        g, d = place[(chip, core)]
        return g * n_dev + d

    def mirrored(chip):
        other = planes[1][0][flat[0]]
        return tuple(other if a == flat[0] else v for a, v in enumerate(chip))

    if any((mirrored(c), k) not in place or (c, k) not in place for c in order for k in range(2)):
        return None
    if any(place[(c, k)][0] != place[(mirrored(c), k)][0] for c in order for k in range(2)):
        return None
    clockwise, counter, mirror, partner = [], [], [], []
    for here in range(length):
        after = (here + 1) % length
        for core in range(2):
            for turn in (lambda c: c, mirrored):
                a, b = index(turn(order[here]), core), index(turn(order[after]), core)
                clockwise.append((a, b))
                counter.append((b, a))
                partner.append((a, index(turn(order[here]), 1 - core)))
            a, b = index(order[here], core), index(mirrored(order[here]), core)
            mirror += [(a, b), (b, a)]
    if any(mate != one ^ n_dev for one, mate in partner):
        return None
    return Rings(length, clockwise, counter, mirror, partner)


def pack_kernel(ids_hbm, gates_hbm, tokens_hbm, out_ref, ids_ref, gates_ref, sem, *, experts):
    count, width = tokens_hbm.shape
    picks = ids_ref.shape[0]
    copies = [
        pltpu.make_async_copy(tokens_hbm, out_ref.at[pl.ds(0, count)], sem.at[0]),
        pltpu.make_async_copy(ids_hbm, ids_ref, sem.at[1]),
        pltpu.make_async_copy(gates_hbm, gates_ref, sem.at[2]),
    ]
    for copy in copies:
        copy.start()
    row = lax.broadcasted_iota(jnp.int32, (experts, count), 0)
    table = jnp.zeros((experts, count), jnp.float32)
    copies[1].wait()
    copies[2].wait()
    ids = ids_ref[...]
    gates = gates_ref[...].astype(jnp.float32)
    for k in range(picks):
        table += jnp.where(ids[k : k + 1, :] == row, gates[k : k + 1, :], 0.0)
    twice = jnp.concatenate([table, table], axis=1).astype(jnp.bfloat16)
    out_ref[count:, :] = jnp.zeros((SUB, width), jnp.bfloat16)
    for q in range(experts // SUB):
        out_ref[count:, q * LANES : (q + 1) * LANES] = twice[q * SUB : (q + 1) * SUB, :]
    copies[0].wait()


def pack(ids, gates, tokens, experts):
    count, width = tokens.shape
    picks = ids.shape[1]
    return pl.pallas_call(
        functools.partial(pack_kernel, experts=experts),
        in_specs=[pl.BlockSpec(memory_space=pltpu.HBM)] * 3,
        out_shape=jax.ShapeDtypeStruct((count + SUB, width), jnp.bfloat16),
        scratch_shapes=[
            pltpu.VMEM((picks, count), jnp.int32),
            pltpu.VMEM((picks, count), jnp.bfloat16),
            pltpu.SemaphoreType.DMA((3,)),
        ],
        name="pack",
        compiler_params=pltpu.CompilerParams(vmem_limit_bytes=2 * MIB),
    )(*(pltpu.with_memory_space_constraint(x, pltpu.HBM) for x in (ids.T, gates.T, tokens)))


def one_hot(seat, cap):
    seats = lax.broadcasted_iota(jnp.int32, (cap, LANES), 0)
    return jnp.where(seats == seat, 1.0, 0.0)


def select_kernel(*refs, count, cap, stride, lent):
    here = lax.axis_index("grp") * stride + lax.axis_index("dev")
    mate = here ^ stride
    out_ref, seat_ref, gate_ref = refs[-3:]
    each = count + SUB
    pieces = [(r, at) for r in refs[:-3] for at in range(0, r.shape[0], each)]
    blocks = len(pieces)
    pairs = blocks // 2
    dot = functools.partial(jnp.dot, preferred_element_type=jnp.float32)
    tails = jnp.concatenate([r[at + count : at + each, :] for r, at in pieces], axis=0)
    upper = (
        lax.broadcasted_iota(jnp.int32, (LANES, LANES), 0)
        < lax.broadcasted_iota(jnp.int32, (LANES, LANES), 1)
    ).astype(jnp.bfloat16)
    before = (
        lax.broadcasted_iota(jnp.int32, (pairs, pairs), 1)
        < lax.broadcasted_iota(jnp.int32, (pairs, pairs), 0)
    ).astype(jnp.bfloat16)
    lane = lax.broadcasted_iota(jnp.int32, (pairs, LANES), 1)
    row_of = lax.broadcasted_iota(jnp.int32, (pairs, blocks * SUB), 0)
    col_of = lax.broadcasted_iota(jnp.int32, (pairs, blocks * SUB), 1)
    groups = tails.shape[1] // LANES
    rows = jnp.concatenate([r[at : at + count, :] for r, at in pieces], axis=0)
    expert = mate if lent else here
    sub = expert % SUB
    group = expert // SUB
    table = tails[:, :LANES]
    for q in range(1, groups):
        table = jnp.where(group == q, tails[:, q * LANES : (q + 1) * LANES], table)
    pick_a = (col_of == (2 * row_of) * SUB + sub).astype(jnp.bfloat16)
    pick_b = (col_of == (2 * row_of + 1) * SUB + sub).astype(jnp.bfloat16)
    gate = jnp.where(lane < count, dot(pick_a, table), dot(pick_b, table))
    chosen = gate > 0.0
    ones = jnp.where(chosen, 1.0, 0.0)
    total = jnp.broadcast_to(jnp.sum(ones, axis=1, keepdims=True), (pairs, LANES))
    spot = dot(ones.astype(jnp.bfloat16), upper) + dot(before, total.astype(jnp.bfloat16))
    spot = spot.astype(jnp.int32)
    seat = jnp.where(here < mate, spot, cap - 1 - spot)
    seat = jnp.where(chosen, seat, -1)
    seat_ref[...] = seat
    gate_ref[...] = gate
    hot = jnp.concatenate([one_hot(seat[o : o + 1, :], cap) for o in range(pairs)], axis=1)
    out_ref[...] = dot(hot.astype(jnp.bfloat16), rows).astype(jnp.bfloat16)


def select(blocks, count, cap, stride, lent):
    width = blocks[0].shape[1]
    pairs = sum(b.shape[0] for b in blocks) // (2 * (count + SUB))
    return pl.pallas_call(
        functools.partial(select_kernel, count=count, cap=cap, stride=stride, lent=lent),
        in_specs=[pl.BlockSpec(memory_space=pltpu.VMEM)] * len(blocks),
        out_shape=[
            jax.ShapeDtypeStruct((cap, width), jnp.bfloat16),
            jax.ShapeDtypeStruct((pairs, LANES), jnp.int32),
            jax.ShapeDtypeStruct((pairs, LANES), jnp.float32),
        ],
        name="select",
        compiler_params=pltpu.CompilerParams(vmem_limit_bytes=16 * MIB),
    )(*blocks)


def load_kernel(source, out_ref, sems, *, at):
    pieces = sems.shape[0]
    rows = out_ref.shape[0] // pieces
    copies = [
        pltpu.make_async_copy(
            source.at[0, pl.ds(at[0] + p * rows, rows), pl.ds(at[1], out_ref.shape[1])],
            out_ref.at[pl.ds(p * rows, rows)],
            sems.at[p],
        )
        for p in range(pieces)
    ]
    for copy in copies:
        copy.start()
    for copy in copies:
        copy.wait()


def load(weights, at, shape):
    return pl.pallas_call(
        functools.partial(load_kernel, at=at),
        in_specs=[pl.BlockSpec(memory_space=pltpu.HBM)],
        out_shape=jax.ShapeDtypeStruct(shape, weights.dtype),
        scratch_shapes=[pltpu.SemaphoreType.DMA((8,))],
        name="load",
        compiler_params=pltpu.CompilerParams(vmem_limit_bytes=4 * MIB),
    )(pltpu.with_memory_space_constraint(weights, pltpu.HBM))


def expert_kernel(own_ref, came_ref, in_a, out_a, out_ref):
    dot = functools.partial(jnp.dot, preferred_element_type=jnp.float32)
    rows = own_ref[...] + came_ref[...]
    result = None
    for first, second in ((in_a, out_a),):
        hidden = jnp.maximum(dot(rows, first[...]), 0.0).astype(jnp.bfloat16)
        part = dot(hidden, second[...])
        result = part if result is None else result + part
    out_ref[...] = result.astype(jnp.bfloat16)


def expert(own, came, weights):
    vmem = pl.BlockSpec(memory_space=pltpu.VMEM)
    return pl.pallas_call(
        expert_kernel,
        in_specs=[vmem] * (2 + len(weights)),
        out_shape=jax.ShapeDtypeStruct(own.shape, jnp.bfloat16),
        name="expert",
        compiler_params=pltpu.CompilerParams(vmem_limit_bytes=16 * MIB),
    )(own, came, *weights)


def spread_kernel(*refs, cap):
    out_refs = refs[6:]
    value = None
    for ref, seat_ref, gate_ref in (refs[:3], refs[3:6]):
        weights = jnp.concatenate(
            [
                one_hot(seat_ref[o : o + 1, :], cap) * gate_ref[o : o + 1, :]
                for o in range(seat_ref.shape[0])
            ],
            axis=1,
        ).astype(jnp.bfloat16)
        part = lax.dot_general(
            weights, ref[...], (((0,), (0,)), ((), ())), preferred_element_type=jnp.float32
        )
        value = part if value is None else value + part
    value = value.astype(jnp.bfloat16)
    at = 0
    for out_ref in out_refs:
        out_ref[...] = value[at : at + out_ref.shape[0], :]
        at += out_ref.shape[0]


def spread(own, came, sizes):
    cap, width = own[0].shape
    return pl.pallas_call(
        functools.partial(spread_kernel, cap=cap),
        out_shape=[jax.ShapeDtypeStruct((size, width), jnp.bfloat16) for size in sizes],
        name="spread",
        compiler_params=pltpu.CompilerParams(vmem_limit_bytes=12 * MIB),
    )(*own, *came)


def on_rings(rings, tokens, expert_ids, gates, w_in, w_out):
    axes = ("grp", "dev")
    n_dev = lax.axis_size("dev")
    experts = lax.axis_size("grp") * n_dev
    count, width = tokens.shape
    length = rings.length
    if 2 * count != LANES or length % 4 or experts % SUB or experts * LANES > SUB * width:
        return per_device(tokens, expert_ids, gates, w_in, w_out)
    inverse = (rings.perms[1], rings.perms[0], rings.perms[2])
    own = pack(expert_ids, gates, tokens, experts)
    each = own.shape[0]
    held = {(0, 0): (own, 0)}
    arrays = [[(own, ((0, 0),))], []]

    def one(block):
        array, at = held[block]
        return array if array.shape[0] == each else array[at : at + each]

    for channel, blocks in gather_sequence():
        source = [one(seen_from_source(channel, b, length)) for b in blocks]
        source = source[0] if len(source) == 1 else jnp.concatenate(source, axis=0)
        came = lax.ppermute(source, axes, rings.perms[channel])
        arrays[blocks[0][1]].append((came, blocks))
        held.update({b: (came, i * each) for i, b in enumerate(blocks)})
    cap = 4 * count
    units = w_in.shape[2]
    weights = []
    for array, at, shape in (
        (w_in, (0, 0), (width, units)),
        (w_out, (0, 0), (units, width)),
    ):
        weights.append(load(array, at, shape))
    parts = {}
    for plane in range(2):
        blocks = [b for _, some in arrays[plane] for b in some]
        pieces = [array for array, _ in arrays[plane]]
        other, *their_seats = select(pieces, count, cap, n_dev, True)
        came = lax.ppermute(other, axes, rings.partner)
        mine, *my_seats = select(pieces, count, cap, n_dev, False)
        result = expert(mine, came, weights)
        theirs = lax.ppermute(result, axes, rings.partner)
        sums = spread((result, *my_seats), (theirs, *their_seats), [count] * len(blocks))
        for block, value in zip(blocks, sums, strict=True):
            parts[block] = [value]

    def total(block):
        value = parts[block][0].astype(jnp.float32)
        for more in parts[block][1:]:
            value = value + more.astype(jnp.float32)
        return value.astype(jnp.bfloat16)

    for channel, blocks in return_sequence():
        source = [total(b) for b in blocks]
        source = source[0] if len(source) == 1 else jnp.concatenate(source, axis=0)
        came = lax.ppermute(source, axes, inverse[channel])
        for i, block in enumerate(blocks):
            piece = came if len(blocks) == 1 else came[i * count : (i + 1) * count]
            parts[seen_from_source(channel, block, length)].append(piece)
    return total((0, 0))


def earlier_count(onehot):
    return jnp.cumsum(onehot, axis=0) - onehot


def contract_rows(left, right):
    return lax.dot_general(
        left,
        right,
        (((0,), (0,)), ((), ())),
        precision=lax.Precision.HIGHEST,
        preferred_element_type=jnp.float32,
    )


def expert_rows(slot_block, w_first, w_second):

    def one_block(rows_block):
        hidden = jnp.maximum(
            jnp.dot(rows_block, w_first, preferred_element_type=jnp.float32), 0.0
        ).astype(jnp.bfloat16)
        return jnp.dot(hidden, w_second, preferred_element_type=jnp.float32).astype(jnp.bfloat16)

    return lax.map(one_block, slot_block)


def seat_sources(seat_of, valid, seat_total):
    item_count = seat_of.shape[0]
    target_seat = jnp.where(valid, seat_of, seat_total)
    empty_seats = jnp.full((seat_total,), item_count, jnp.int32)
    return empty_seats.at[target_seat].set(jnp.arange(item_count, dtype=jnp.int32), mode="drop")


def per_device(tokens, expert_ids, gates, w_in, w_out):
    n_grp = lax.axis_size("grp")
    n_dev = lax.axis_size("dev")
    token_count, feature_width = tokens.shape
    cap_grp = min(token_count, 3 * ((4 * token_count + n_grp - 1) // n_grp))
    cap_exp = min(4 * token_count, 24 * token_count // n_dev)
    seat_total = n_dev * cap_exp
    zero_half = jnp.zeros((), jnp.bfloat16)
    w_first = w_in[0]
    w_second = w_out[0]
    pair_ids = expert_ids.reshape(token_count * 4, 2)
    pair_group = pair_ids[:, 0] // n_dev
    group_hot = (pair_group[:, None] == jnp.arange(n_grp)[None, :]).astype(jnp.int32)
    group_rank = jnp.sum(earlier_count(group_hot) * group_hot, axis=1)
    target = pair_group * cap_grp + group_rank
    slot_count = n_grp * cap_grp
    placed = (target[None, :] == jnp.arange(slot_count)[:, None]).astype(jnp.int32)
    token_hot = placed.reshape(slot_count, token_count, 4).sum(axis=2)
    rows_out = jnp.dot(
        token_hot.astype(jnp.bfloat16), tokens, preferred_element_type=jnp.float32
    ).astype(jnp.bfloat16)
    local_ids = pair_ids % n_dev
    picks_out = jnp.dot(placed, local_ids + 1) - 1
    gains_out = jnp.dot(
        placed.astype(jnp.bfloat16),
        gates.reshape(token_count * 4, 2),
        preferred_element_type=jnp.float32,
    ).astype(jnp.bfloat16)
    rows_in, picks_in, gains_in = (
        lax.all_to_all(
            rows_out.reshape(n_grp, cap_grp, feature_width),
            "grp",
            split_axis=0,
            concat_axis=0,
            tiled=True,
        ),
        lax.all_to_all(
            picks_out.reshape(n_grp, cap_grp, 2), "grp", split_axis=0, concat_axis=0, tiled=True
        ),
        lax.all_to_all(
            gains_out.reshape(n_grp, cap_grp, 2), "grp", split_axis=0, concat_axis=0, tiled=True
        ),
    )
    relay_rows = rows_in.reshape(slot_count, feature_width)
    relay_picks = picks_in.reshape(slot_count, 2)
    relay_gains = gains_in.reshape(slot_count, 2)
    live_count = 4 * token_count
    slot_live = (relay_picks[:, 0] >= 0).astype(jnp.int32)
    slot_order = jnp.cumsum(slot_live) - 1
    packed = (
        (slot_order[None, :] == jnp.arange(live_count)[:, None]) & (slot_live[None, :] > 0)
    ).astype(jnp.int32)
    packed_rows = jnp.dot(
        packed.astype(jnp.bfloat16), relay_rows, preferred_element_type=jnp.float32
    ).astype(jnp.bfloat16)
    packed_picks = jnp.dot(packed, relay_picks)
    packed_gains = jnp.dot(
        packed.astype(jnp.bfloat16), relay_gains, preferred_element_type=jnp.float32
    ).astype(jnp.bfloat16)
    group_rows, group_picks, group_gains = (
        lax.all_gather(packed_rows, "dev", axis=0, tiled=True),
        lax.all_gather(packed_picks, "dev", axis=0, tiled=True),
        lax.all_gather(packed_gains, "dev", axis=0, tiled=True),
    )
    gathered_count = group_rows.shape[0]
    chosen = jnp.sum((group_picks == lax.axis_index("dev")).astype(jnp.int32), axis=1)
    expert_seat = jnp.cumsum(chosen) - 1
    seat_source = seat_sources(expert_seat, chosen > 0, seat_total)
    seat_live = seat_source < gathered_count
    taken_rows = jnp.take(group_rows, jnp.minimum(seat_source, gathered_count - 1), axis=0)
    expert_in = jnp.where(seat_live[:, None], taken_rows, zero_half)
    expert_out = expert_rows(
        expert_in.reshape(n_dev, cap_exp, feature_width), w_first, w_second
    ).reshape(seat_total, feature_width)
    spread_rows = jnp.take(expert_out, jnp.clip(expert_seat, 0, seat_total - 1), axis=0)
    spread = jnp.where((chosen > 0)[:, None], spread_rows, zero_half)
    back = lax.all_to_all(
        spread.reshape(n_dev, live_count, feature_width),
        "dev",
        split_axis=0,
        concat_axis=0,
        tiled=True,
    )
    match = (packed_picks[None, :, :] == jnp.arange(n_dev)[:, None, None]).astype(jnp.float32)
    row_weights = jnp.sum(match * packed_gains.astype(jnp.float32)[None, :, :], axis=2)
    packed_sum = jnp.sum(row_weights[:, :, None] * back.astype(jnp.float32), axis=0)
    partial_value = contract_rows(packed.astype(jnp.float32), packed_sum)
    returned_sums = lax.all_to_all(
        partial_value.reshape(n_grp, cap_grp, feature_width),
        "grp",
        split_axis=0,
        concat_axis=0,
        tiled=True,
    )
    mixed = contract_rows(
        token_hot.astype(jnp.float32), returned_sums.reshape(slot_count, feature_width)
    )
    return mixed.astype(jnp.bfloat16)


def solution(mesh):
    rings = find_rings(mesh)
    if rings is None:
        return mapped(mesh, per_device)

    def body(*args):
        return on_rings(rings, *args)

    return mapped(mesh, body)


def mapped(mesh, body):
    return jax.shard_map(
        body,
        mesh=mesh,
        in_specs=(
            P(("grp", "dev"), None),
            P(("grp", "dev"), None),
            P(("grp", "dev"), None),
            P(("grp", "dev"), None, None),
            P(("grp", "dev"), None, None),
        ),
        out_specs=P(("grp", "dev"), None),
        check_vma=False,
    )
```

```python
import functools

import jax
import jax.numpy as jnp
from jax import lax
from jax.experimental import pallas as pl
from jax.experimental.pallas import tpu as pltpu
from jax.sharding import PartitionSpec as P


LANES = 128
SUB = 8
MIB = 1 << 20
RETURN = (
    (2, ((4, 1),)),
    (0, ((-3, 1),)),
    (1, ((3, 1),)),
    (2, ((0, 1),)),
    (0, ((4, 0),)),
    (2, ((-2, 1),)),
    (1, ((2, 1),)),
    (0, ((-3, 0),)),
    (1, ((3, 0),)),
    (2, ((-1, 1),)),
    (0, ((-2, 0),)),
    (1, ((2, 0),)),
    (2, ((1, 1),)),
    (0, ((-1, 0),)),
    (1, ((1, 0),)),
)
GATHER = (
    (0, ((-1, 0),)),
    (1, ((1, 0),)),
    (2, ((0, 1),)),
    (0, ((-2, 0),)),
    (1, ((2, 0),)),
    (2, ((1, 1), (-1, 1),)),
    (0, ((-3, 0),)),
    (1, ((3, 0),)),
    (2, ((2, 1),)),
    (0, ((4, 0),)),
    (2, ((3, 1), (-3, 1),)),
    (0, ((-2, 1),)),
    (2, ((4, 1),)),
)


class Rings:
    def __init__(self, length, clockwise, counter, mirror, partner):
        self.length = length
        self.perms = (clockwise, counter, mirror)
        self.partner = partner


def wrap(step, length):
    step %= length
    return step - length if step > length // 2 else step


def seen_from_source(channel, block, length):
    step, plane = block
    if channel == 0:
        return (wrap(step + 1, length), plane)
    if channel == 1:
        return (wrap(step - 1, length), plane)
    return (step, 1 - plane)


def gather_sequence():
    return GATHER


def return_sequence():
    return RETURN


def find_rings(mesh):
    grid = mesh.devices
    n_grp, n_dev = grid.shape
    if n_dev != 2 or not hasattr(grid[0, 0], "coords"):
        return None
    place = {}
    for g in range(n_grp):
        for d in range(n_dev):
            device = grid[g, d]
            place[(tuple(device.coords), device.core_on_chip)] = (g, d)
    planes = []
    for d in range(n_dev):
        planes.append(sorted({tuple(grid[g, d].coords) for g in range(n_grp)}))
    if 2 * len(planes[0]) != n_grp or set(planes[0]) & set(planes[1]):
        return None
    wide = [a for a in range(3) if len({c[a] for c in planes[0]}) == 2]
    flat = [a for a in range(3) if len({c[a] for c in planes[0]}) == 1]
    if not wide or len(flat) != 1:
        return None
    side = wide[0]
    along = [a for a in range(3) if a not in (side, flat[0])][0]
    low = min(c[side] for c in planes[0])
    up = sorted((c for c in planes[0] if c[side] == low), key=lambda c: c[along])
    down = sorted((c for c in planes[0] if c[side] != low), key=lambda c: -c[along])
    order = up + down
    length = len(order)
    if length != 8:
        return None

    def index(chip, core):
        g, d = place[(chip, core)]
        return g * n_dev + d

    def mirrored(chip):
        other = planes[1][0][flat[0]]
        return tuple(other if a == flat[0] else v for a, v in enumerate(chip))

    if any((mirrored(c), k) not in place or (c, k) not in place for c in order for k in range(2)):
        return None
    if any(place[(c, k)][0] != place[(mirrored(c), k)][0] for c in order for k in range(2)):
        return None
    clockwise, counter, mirror, partner = [], [], [], []
    for here in range(length):
        after = (here + 1) % length
        for core in range(2):
            for turn in (lambda c: c, mirrored):
                a, b = index(turn(order[here]), core), index(turn(order[after]), core)
                clockwise.append((a, b))
                counter.append((b, a))
                partner.append((a, index(turn(order[here]), 1 - core)))
            a, b = index(order[here], core), index(mirrored(order[here]), core)
            mirror += [(a, b), (b, a)]
    if any(mate != one ^ n_dev for one, mate in partner):
        return None
    return Rings(length, clockwise, counter, mirror, partner)


def pack_kernel(ids_hbm, gates_hbm, tokens_hbm, out_ref, ids_ref, gates_ref, sem, *, experts):
    count, width = tokens_hbm.shape
    picks = ids_ref.shape[0]
    copies = [
        pltpu.make_async_copy(tokens_hbm, out_ref.at[pl.ds(0, count)], sem.at[0]),
        pltpu.make_async_copy(ids_hbm, ids_ref, sem.at[1]),
        pltpu.make_async_copy(gates_hbm, gates_ref, sem.at[2]),
    ]
    for copy in copies:
        copy.start()
    row = lax.broadcasted_iota(jnp.int32, (experts, count), 0)
    table = jnp.zeros((experts, count), jnp.float32)
    copies[1].wait()
    copies[2].wait()
    ids = ids_ref[...]
    gates = gates_ref[...].astype(jnp.float32)
    for k in range(picks):
        table += jnp.where(ids[k : k + 1, :] == row, gates[k : k + 1, :], 0.0)
    twice = jnp.concatenate([table, table], axis=1).astype(jnp.bfloat16)
    out_ref[count:, :] = jnp.zeros((SUB, width), jnp.bfloat16)
    for q in range(experts // SUB):
        out_ref[count:, q * LANES : (q + 1) * LANES] = twice[q * SUB : (q + 1) * SUB, :]
    copies[0].wait()


def pack(ids, gates, tokens, experts):
    count, width = tokens.shape
    picks = ids.shape[1]
    return pl.pallas_call(
        functools.partial(pack_kernel, experts=experts),
        in_specs=[pl.BlockSpec(memory_space=pltpu.HBM)] * 3,
        out_shape=jax.ShapeDtypeStruct((count + SUB, width), jnp.bfloat16),
        scratch_shapes=[
            pltpu.VMEM((picks, count), jnp.int32),
            pltpu.VMEM((picks, count), jnp.bfloat16),
            pltpu.SemaphoreType.DMA((3,)),
        ],
        name="pack",
        compiler_params=pltpu.CompilerParams(vmem_limit_bytes=2 * MIB),
    )(*(pltpu.with_memory_space_constraint(x, pltpu.HBM) for x in (ids.T, gates.T, tokens)))


def one_hot(seat, cap):
    seats = lax.broadcasted_iota(jnp.int32, (cap, LANES), 0)
    return jnp.where(seats == seat, 1.0, 0.0)


def select_kernel(*refs, count, cap, stride, lent):
    here = lax.axis_index("grp") * stride + lax.axis_index("dev")
    mate = here ^ stride
    out_ref, seat_ref, gate_ref = refs[-3:]
    each = count + SUB
    pieces = [(r, at) for r in refs[:-3] for at in range(0, r.shape[0], each)]
    blocks = len(pieces)
    pairs = blocks // 2
    dot = functools.partial(jnp.dot, preferred_element_type=jnp.float32)
    tails = jnp.concatenate([r[at + count : at + each, :] for r, at in pieces], axis=0)
    upper = (
        lax.broadcasted_iota(jnp.int32, (LANES, LANES), 0)
        < lax.broadcasted_iota(jnp.int32, (LANES, LANES), 1)
    ).astype(jnp.bfloat16)
    before = (
        lax.broadcasted_iota(jnp.int32, (pairs, pairs), 1)
        < lax.broadcasted_iota(jnp.int32, (pairs, pairs), 0)
    ).astype(jnp.bfloat16)
    lane = lax.broadcasted_iota(jnp.int32, (pairs, LANES), 1)
    row_of = lax.broadcasted_iota(jnp.int32, (pairs, blocks * SUB), 0)
    col_of = lax.broadcasted_iota(jnp.int32, (pairs, blocks * SUB), 1)
    groups = tails.shape[1] // LANES
    rows = jnp.concatenate([r[at : at + count, :] for r, at in pieces], axis=0)
    expert = mate if lent else here
    sub = expert % SUB
    group = expert // SUB
    table = tails[:, :LANES]
    for q in range(1, groups):
        table = jnp.where(group == q, tails[:, q * LANES : (q + 1) * LANES], table)
    pick_a = (col_of == (2 * row_of) * SUB + sub).astype(jnp.bfloat16)
    pick_b = (col_of == (2 * row_of + 1) * SUB + sub).astype(jnp.bfloat16)
    gate = jnp.where(lane < count, dot(pick_a, table), dot(pick_b, table))
    chosen = gate > 0.0
    ones = jnp.where(chosen, 1.0, 0.0)
    total = jnp.broadcast_to(jnp.sum(ones, axis=1, keepdims=True), (pairs, LANES))
    spot = dot(ones.astype(jnp.bfloat16), upper) + dot(before, total.astype(jnp.bfloat16))
    spot = spot.astype(jnp.int32)
    seat = jnp.where(here < mate, spot, cap - 1 - spot)
    seat = jnp.where(chosen, seat, -1)
    seat_ref[...] = seat
    gate_ref[...] = gate
    hot = jnp.concatenate([one_hot(seat[o : o + 1, :], cap) for o in range(pairs)], axis=1)
    out_ref[...] = dot(hot.astype(jnp.bfloat16), rows).astype(jnp.bfloat16)


def select(blocks, count, cap, stride, lent):
    width = blocks[0].shape[1]
    pairs = sum(b.shape[0] for b in blocks) // (2 * (count + SUB))
    return pl.pallas_call(
        functools.partial(select_kernel, count=count, cap=cap, stride=stride, lent=lent),
        in_specs=[pl.BlockSpec(memory_space=pltpu.VMEM)] * len(blocks),
        out_shape=[
            jax.ShapeDtypeStruct((cap, width), jnp.bfloat16),
            jax.ShapeDtypeStruct((pairs, LANES), jnp.int32),
            jax.ShapeDtypeStruct((pairs, LANES), jnp.float32),
        ],
        name="select",
        compiler_params=pltpu.CompilerParams(vmem_limit_bytes=16 * MIB),
    )(*blocks)


def load_kernel(source, out_ref, sems, *, at):
    pieces = sems.shape[0]
    rows = out_ref.shape[0] // pieces
    copies = [
        pltpu.make_async_copy(
            source.at[0, pl.ds(at[0] + p * rows, rows), pl.ds(at[1], out_ref.shape[1])],
            out_ref.at[pl.ds(p * rows, rows)],
            sems.at[p],
        )
        for p in range(pieces)
    ]
    for copy in copies:
        copy.start()
    for copy in copies:
        copy.wait()


def load(weights, at, shape):
    return pl.pallas_call(
        functools.partial(load_kernel, at=at),
        in_specs=[pl.BlockSpec(memory_space=pltpu.HBM)],
        out_shape=jax.ShapeDtypeStruct(shape, weights.dtype),
        scratch_shapes=[pltpu.SemaphoreType.DMA((8,))],
        name="load",
        compiler_params=pltpu.CompilerParams(vmem_limit_bytes=4 * MIB),
    )(pltpu.with_memory_space_constraint(weights, pltpu.HBM))


def expert_kernel(own_ref, came_ref, in_a, out_a, out_ref):
    dot = functools.partial(jnp.dot, preferred_element_type=jnp.float32)
    rows = own_ref[...] + came_ref[...]
    result = None
    for first, second in ((in_a, out_a),):
        hidden = jnp.maximum(dot(rows, first[...]), 0.0).astype(jnp.bfloat16)
        part = dot(hidden, second[...])
        result = part if result is None else result + part
    out_ref[...] = result.astype(jnp.bfloat16)


def expert(own, came, weights):
    vmem = pl.BlockSpec(memory_space=pltpu.VMEM)
    return pl.pallas_call(
        expert_kernel,
        in_specs=[vmem] * (2 + len(weights)),
        out_shape=jax.ShapeDtypeStruct(own.shape, jnp.bfloat16),
        name="expert",
        compiler_params=pltpu.CompilerParams(vmem_limit_bytes=16 * MIB),
    )(own, came, *weights)


def spread_kernel(*refs, cap, some):
    out_refs = refs[6:]
    value = None
    for ref, seat_ref, gate_ref in (refs[:3], refs[3:6]):
        weights = jnp.concatenate(
            [
                one_hot(seat_ref[o : o + 1, :], cap) * gate_ref[o : o + 1, :]
                for o in some
            ],
            axis=1,
        ).astype(jnp.bfloat16)
        part = lax.dot_general(
            weights, ref[...], (((0,), (0,)), ((), ())), preferred_element_type=jnp.float32
        )
        value = part if value is None else value + part
    value = value.astype(jnp.bfloat16)
    at = 0
    for out_ref in out_refs:
        out_ref[...] = value[at : at + out_ref.shape[0], :]
        at += out_ref.shape[0]


def spread(own, came, sizes, some):
    cap, width = own[0].shape
    return pl.pallas_call(
        functools.partial(spread_kernel, cap=cap, some=some),
        out_shape=[jax.ShapeDtypeStruct((size, width), jnp.bfloat16) for size in sizes],
        name="spread",
        compiler_params=pltpu.CompilerParams(vmem_limit_bytes=12 * MIB),
    )(*own, *came)


def on_rings(rings, tokens, expert_ids, gates, w_in, w_out):
    axes = ("grp", "dev")
    n_dev = lax.axis_size("dev")
    experts = lax.axis_size("grp") * n_dev
    count, width = tokens.shape
    length = rings.length
    if 2 * count != LANES or length % 4 or experts % SUB or experts * LANES > SUB * width:
        return per_device(tokens, expert_ids, gates, w_in, w_out)
    inverse = (rings.perms[1], rings.perms[0], rings.perms[2])
    own = pack(expert_ids, gates, tokens, experts)
    each = own.shape[0]
    held = {(0, 0): (own, 0)}
    arrays = [[(own, ((0, 0),))], []]

    def one(block):
        array, at = held[block]
        return array if array.shape[0] == each else array[at : at + each]

    for channel, blocks in gather_sequence():
        source = [one(seen_from_source(channel, b, length)) for b in blocks]
        source = source[0] if len(source) == 1 else jnp.concatenate(source, axis=0)
        came = lax.ppermute(source, axes, rings.perms[channel])
        arrays[blocks[0][1]].append((came, blocks))
        held.update({b: (came, i * each) for i, b in enumerate(blocks)})
    cap = 4 * count
    units = w_in.shape[2]
    weights = []
    for array, at, shape in (
        (w_in, (0, 0), (width, units)),
        (w_out, (0, 0), (units, width)),
    ):
        weights.append(load(array, at, shape))
    parts = {}
    for plane in range(2):
        blocks = [b for _, some in arrays[plane] for b in some]
        pieces = [array for array, _ in arrays[plane]]
        other, *their_seats = select(pieces, count, cap, n_dev, True)
        came = lax.ppermute(other, axes, rings.partner)
        mine, *my_seats = select(pieces, count, cap, n_dev, False)
        result = expert(mine, came, weights)
        theirs = lax.ppermute(result, axes, rings.partner)
        pairs = len(blocks) // 2
        cut = pairs // 2 if plane else 0
        both = ((result, *my_seats), (theirs, *their_seats))
        sums = spread(*both, [count] * (2 * (pairs - cut)), range(cut, pairs))
        if cut:
            sums = spread(*both, [count] * (2 * cut), range(cut)) + sums
        for block, value in zip(blocks, sums, strict=True):
            parts[block] = [value]

    def total(block):
        value = parts[block][0].astype(jnp.float32)
        for more in parts[block][1:]:
            value = value + more.astype(jnp.float32)
        return value.astype(jnp.bfloat16)

    for channel, blocks in return_sequence():
        source = [total(b) for b in blocks]
        source = source[0] if len(source) == 1 else jnp.concatenate(source, axis=0)
        came = lax.ppermute(source, axes, inverse[channel])
        for i, block in enumerate(blocks):
            piece = came if len(blocks) == 1 else came[i * count : (i + 1) * count]
            parts[seen_from_source(channel, block, length)].append(piece)
    return total((0, 0))


def earlier_count(onehot):
    return jnp.cumsum(onehot, axis=0) - onehot


def contract_rows(left, right):
    return lax.dot_general(
        left,
        right,
        (((0,), (0,)), ((), ())),
        precision=lax.Precision.HIGHEST,
        preferred_element_type=jnp.float32,
    )


def expert_rows(slot_block, w_first, w_second):

    def one_block(rows_block):
        hidden = jnp.maximum(
            jnp.dot(rows_block, w_first, preferred_element_type=jnp.float32), 0.0
        ).astype(jnp.bfloat16)
        return jnp.dot(hidden, w_second, preferred_element_type=jnp.float32).astype(jnp.bfloat16)

    return lax.map(one_block, slot_block)


def seat_sources(seat_of, valid, seat_total):
    item_count = seat_of.shape[0]
    target_seat = jnp.where(valid, seat_of, seat_total)
    empty_seats = jnp.full((seat_total,), item_count, jnp.int32)
    return empty_seats.at[target_seat].set(jnp.arange(item_count, dtype=jnp.int32), mode="drop")


def per_device(tokens, expert_ids, gates, w_in, w_out):
    n_grp = lax.axis_size("grp")
    n_dev = lax.axis_size("dev")
    token_count, feature_width = tokens.shape
    cap_grp = min(token_count, 3 * ((4 * token_count + n_grp - 1) // n_grp))
    cap_exp = min(4 * token_count, 24 * token_count // n_dev)
    seat_total = n_dev * cap_exp
    zero_half = jnp.zeros((), jnp.bfloat16)
    w_first = w_in[0]
    w_second = w_out[0]
    pair_ids = expert_ids.reshape(token_count * 4, 2)
    pair_group = pair_ids[:, 0] // n_dev
    group_hot = (pair_group[:, None] == jnp.arange(n_grp)[None, :]).astype(jnp.int32)
    group_rank = jnp.sum(earlier_count(group_hot) * group_hot, axis=1)
    target = pair_group * cap_grp + group_rank
    slot_count = n_grp * cap_grp
    placed = (target[None, :] == jnp.arange(slot_count)[:, None]).astype(jnp.int32)
    token_hot = placed.reshape(slot_count, token_count, 4).sum(axis=2)
    rows_out = jnp.dot(
        token_hot.astype(jnp.bfloat16), tokens, preferred_element_type=jnp.float32
    ).astype(jnp.bfloat16)
    local_ids = pair_ids % n_dev
    picks_out = jnp.dot(placed, local_ids + 1) - 1
    gains_out = jnp.dot(
        placed.astype(jnp.bfloat16),
        gates.reshape(token_count * 4, 2),
        preferred_element_type=jnp.float32,
    ).astype(jnp.bfloat16)
    rows_in, picks_in, gains_in = (
        lax.all_to_all(
            rows_out.reshape(n_grp, cap_grp, feature_width),
            "grp",
            split_axis=0,
            concat_axis=0,
            tiled=True,
        ),
        lax.all_to_all(
            picks_out.reshape(n_grp, cap_grp, 2), "grp", split_axis=0, concat_axis=0, tiled=True
        ),
        lax.all_to_all(
            gains_out.reshape(n_grp, cap_grp, 2), "grp", split_axis=0, concat_axis=0, tiled=True
        ),
    )
    relay_rows = rows_in.reshape(slot_count, feature_width)
    relay_picks = picks_in.reshape(slot_count, 2)
    relay_gains = gains_in.reshape(slot_count, 2)
    live_count = 4 * token_count
    slot_live = (relay_picks[:, 0] >= 0).astype(jnp.int32)
    slot_order = jnp.cumsum(slot_live) - 1
    packed = (
        (slot_order[None, :] == jnp.arange(live_count)[:, None]) & (slot_live[None, :] > 0)
    ).astype(jnp.int32)
    packed_rows = jnp.dot(
        packed.astype(jnp.bfloat16), relay_rows, preferred_element_type=jnp.float32
    ).astype(jnp.bfloat16)
    packed_picks = jnp.dot(packed, relay_picks)
    packed_gains = jnp.dot(
        packed.astype(jnp.bfloat16), relay_gains, preferred_element_type=jnp.float32
    ).astype(jnp.bfloat16)
    group_rows, group_picks, group_gains = (
        lax.all_gather(packed_rows, "dev", axis=0, tiled=True),
        lax.all_gather(packed_picks, "dev", axis=0, tiled=True),
        lax.all_gather(packed_gains, "dev", axis=0, tiled=True),
    )
    gathered_count = group_rows.shape[0]
    chosen = jnp.sum((group_picks == lax.axis_index("dev")).astype(jnp.int32), axis=1)
    expert_seat = jnp.cumsum(chosen) - 1
    seat_source = seat_sources(expert_seat, chosen > 0, seat_total)
    seat_live = seat_source < gathered_count
    taken_rows = jnp.take(group_rows, jnp.minimum(seat_source, gathered_count - 1), axis=0)
    expert_in = jnp.where(seat_live[:, None], taken_rows, zero_half)
    expert_out = expert_rows(
        expert_in.reshape(n_dev, cap_exp, feature_width), w_first, w_second
    ).reshape(seat_total, feature_width)
    spread_rows = jnp.take(expert_out, jnp.clip(expert_seat, 0, seat_total - 1), axis=0)
    spread = jnp.where((chosen > 0)[:, None], spread_rows, zero_half)
    back = lax.all_to_all(
        spread.reshape(n_dev, live_count, feature_width),
        "dev",
        split_axis=0,
        concat_axis=0,
        tiled=True,
    )
    match = (packed_picks[None, :, :] == jnp.arange(n_dev)[:, None, None]).astype(jnp.float32)
    row_weights = jnp.sum(match * packed_gains.astype(jnp.float32)[None, :, :], axis=2)
    packed_sum = jnp.sum(row_weights[:, :, None] * back.astype(jnp.float32), axis=0)
    partial_value = contract_rows(packed.astype(jnp.float32), packed_sum)
    returned_sums = lax.all_to_all(
        partial_value.reshape(n_grp, cap_grp, feature_width),
        "grp",
        split_axis=0,
        concat_axis=0,
        tiled=True,
    )
    mixed = contract_rows(
        token_hot.astype(jnp.float32), returned_sums.reshape(slot_count, feature_width)
    )
    return mixed.astype(jnp.bfloat16)


def solution(mesh):
    rings = find_rings(mesh)
    if rings is None:
        return mapped(mesh, per_device)

    def body(*args):
        return on_rings(rings, *args)

    return mapped(mesh, body)


def mapped(mesh, body):
    return jax.shard_map(
        body,
        mesh=mesh,
        in_specs=(
            P(("grp", "dev"), None),
            P(("grp", "dev"), None),
            P(("grp", "dev"), None),
            P(("grp", "dev"), None, None),
            P(("grp", "dev"), None, None),
        ),
        out_specs=P(("grp", "dev"), None),
        check_vma=False,
    )
```
